32 devices in a mesh: seq: 16 (over z, x, core), tp: 2 (over y).
Axes of the slice: x: 2, y: 2, z: 4, core: 2. Of those that a mesh axis runs over, the one named last changes fastest.
Arguments:
- tokens: bfloat16 [8192, 4096], P('seq'), may hold values from -6 to 6
- w_in: bfloat16 [4096, 3, 4096], P('seq', None, 'tp'), may hold values from -0.09375 to 0.09375
- short_taps: float32 [3, 3, 4096], P(None, None, 'tp'), may hold values from -3 to 3
- decay_rate: float32 [256, 16], P('tp'), may hold values from 1.2207031e-05 to 0.04, as said below
- residue: float32 [256, 16], P('tp'), may hold values from -4 to 4
- skip_gain: float32 [4096], P('tp'), may hold values from -4 to 4
- w_out: bfloat16 [4096, 4096], P('tp'), may hold values from -0.125 to 0.125
Outputs:
- mixed: bfloat16 [8192, 4096], P('seq', 'tp')
The draws below stay inside these ranges and needn't reach their ends.
Inputs may be any that keep to these rules, and one draw needn't show every extreme that they name: `decay_rate`: every decay rate is positive.
All inputs are finite; a program needn't handle non-finite values.
Results may differ from the reference program's by a relative error of at most 0.0075.
Values may be sent and summed in bfloat16 or wider, within the bound.
A program may use at most 192 MiB of HBM per device.

```python
import math
import jax
import jax.numpy as jnp
from jax import lax

D = 4096
ORDER = 16
FILTER_WIDTH = 16
TAPS = 3
LENGTH = 8192
GROUPS = 256
N_TP = 2


def draw_decay_rate(key, part):
    first, second, third = jax.random.split(key, 3)
    share = 0.5
    coin = jax.random.uniform(first, (GROUPS, ORDER), jnp.float32) < share
    slow = jnp.exp(jax.random.uniform(second, (GROUPS, ORDER), jnp.float32, math.log(0.1 / LENGTH), math.log(2.0 / LENGTH)))
    fast = jnp.exp(jax.random.uniform(third, (GROUPS, ORDER), jnp.float32, math.log(0.01), math.log(0.04)))
    return jnp.clip(jnp.where(coin, fast, slow), 0.1 / LENGTH, 0.04).astype(jnp.float32)


def spiked(result, stream_key, source, target, blocks, factor):
    owner, partner = [(jnp.arange(result.shape[position]) // (result.shape[position] // blocks)).reshape([-1 if axis == position else 1 for axis in range(result.ndim)]) for position in (source, target)]
    chosen = jax.random.permutation(stream_key, blocks)[partner]
    strong = (owner == chosen) | (owner == (partner + blocks // 2) % blocks)
    return jnp.where(strong, factor * result, result)


def steps_of(own_key, extent, pieces, least, largest):
    gain = 1.0
    for position, shards_of in pieces:
        heights = jax.random.uniform(jax.random.fold_in(jax.random.fold_in(own_key, 6), position), (shards_of,), jnp.float32, least / len(pieces), largest / len(pieces))
        gain = gain * jnp.repeat(jnp.exp(heights), extent[position] // shards_of).reshape((-1,) + (1,) * (len(extent) - 1 - position))
    return gain


def gaussian(own_key, extent, width, limit, pieces=(), held_as=jnp.bfloat16):
    level = steps_of(own_key, extent, pieces, -0.22, 0.18) if pieces else 1.0
    array = jax.random.normal(own_key, extent, jnp.float32) * width * level
    return jnp.minimum(jnp.maximum(array, -limit), limit).astype(held_as)


def gaussian_with(rng, extent, spread, bound, cuts, heavy, kind=jnp.bfloat16):
    values = spread * jax.random.normal(rng, extent, jnp.float32)
    if cuts:
        values = values * steps_of(rng, extent, cuts, -0.22, 0.18)
    return jnp.clip(spiked(values, jax.random.fold_in(rng, 3), *heavy), -bound, bound).astype(kind)


def setup_inputs(seed: int = 0) -> dict:
    arg_keys = jax.random.split(jax.random.key(seed), 8)
    return {
        "tokens": gaussian(arg_keys[0], (LENGTH, D), 1.0, 6.0, ((0, 16),)),
        "w_in": gaussian(arg_keys[1], (D, 3, D), D ** -0.5, 0.09375, ((0, 16), (2, 2))),
        "short_taps": gaussian(arg_keys[2], (TAPS, 3, D), 0.6, 3.0, ((2, 2),), jnp.float32),
        "decay_rate": draw_decay_rate(jax.random.fold_in(arg_keys[7], 71), 0),
        "residue": gaussian(arg_keys[4], (GROUPS, ORDER), 1.0, 4.0, ((0, 2),), jnp.float32),
        "skip_gain": gaussian(arg_keys[5], (D,), 1.0, 4.0, ((0, 2),), jnp.float32),
        "w_out": gaussian_with(arg_keys[6], (D, D), D ** -0.5, 0.125, ((0, 2),), (0, 1, 2, 2.0)),
    }


def reference(tokens, w_in, short_taps, decay_rate, residue, skip_gain, w_out):
    proj = jnp.dot(tokens, w_in.reshape(D, 3 * D), preferred_element_type=jnp.float32)
    proj = proj.astype(jnp.bfloat16).reshape(LENGTH, 3, D).astype(jnp.float32)
    padded = jnp.concatenate([jnp.zeros((TAPS - 1, 3, D), jnp.float32), proj], axis=0)
    filtered = jnp.zeros((LENGTH, 3, D), jnp.float32)
    for tap in range(TAPS):
        filtered = filtered + short_taps[tap] * padded[TAPS - 1 - tap:TAPS - 1 - tap + LENGTH]
    query = filtered[:, 0]
    gated = filtered[:, 1] * filtered[:, 2]
    decay = jnp.repeat(jnp.exp(-decay_rate), FILTER_WIDTH, axis=0).T
    weight_mode = jnp.repeat(residue * jnp.sqrt(2.0 * decay_rate / ORDER), FILTER_WIDTH, axis=0).T

    def advance(state, value):
        state = decay * state + value[None, :]
        return (state, lax.optimization_barrier(jnp.sum(weight_mode * state, axis=0)))
    _, conv = lax.scan(advance, jnp.zeros((ORDER, D), jnp.float32), gated)
    mix = (query * (conv + skip_gain * gated)).astype(jnp.bfloat16)
    share = D // N_TP
    total = jnp.zeros((LENGTH, D), jnp.float32)
    for block in range(N_TP):
        partial_value = jnp.dot(mix[:, block * share:(block + 1) * share], w_out[block * share:(block + 1) * share], preferred_element_type=jnp.float32)
        partial_value = lax.optimization_barrier(partial_value.astype(jnp.bfloat16))
        total = total + partial_value.astype(jnp.float32)
    return total.astype(jnp.bfloat16)
```

```python
import functools

import jax
import jax.numpy as jnp
from jax import lax
from jax.experimental import pallas as pl
from jax.experimental.pallas import tpu as pltpu
from jax.sharding import PartitionSpec as P

SUB = 128
LANES = 256
BLOCK = 128
HALO = 16
MESH = pl.DeviceIdType.MESH
HIGHEST = lax.Precision.HIGHEST


def shifted_by(block, axis, distance):
    devices = range(lax.axis_size(axis))
    route = [(i - distance, i) for i in devices if i - distance in devices]
    return lax.ppermute(block, axis, route)


def fanned(state, width, order):
    lanes = state.shape[1]
    tile = lanes // width
    full = jnp.concatenate([state] * tile, axis=0)
    row = lax.broadcasted_iota(jnp.int32, full.shape, 0) // order
    lane = lax.broadcasted_iota(jnp.int32, full.shape, 1) // width
    return jnp.where(row == lane, full, 0.0)


def split(value):
    high = value.astype(jnp.bfloat16)
    return high, (value - high.astype(jnp.float32)).astype(jnp.bfloat16)


def product3(a, b):
    (ah, al), (bh, bl) = split(a), split(b)
    dot = functools.partial(jnp.dot, preferred_element_type=jnp.float32)
    return dot(ah, bh) + (dot(ah, bl) + dot(al, bh))


def conv_kernel(
    width, q_ref, k_ref, v_ref, taps_ref, lags_ref, leave_ref, reach_ref, fade_ref, skip_ref,
    query_ref, base_ref, state_ref, toep_ref
):
    taps = taps_ref.shape[0]
    count, lanes = query_ref.shape
    order = state_ref.shape[0]
    tile = lanes // width

    def filtered(ref, which):
        value = ref[...].astype(jnp.float32)
        total = None
        for tap in range(taps):
            term = taps_ref[tap, which][None, :] * value[HALO - tap : HALO - tap + count]
            total = term if total is None else total + term
        return total

    query_ref[...] = filtered(q_ref, 0)
    gated = filtered(k_ref, 1) * filtered(v_ref, 2)
    lane = lax.broadcasted_iota(jnp.int32, (SUB, lanes), 1) // width
    row = lax.broadcasted_iota(jnp.int32, (tile * order, lanes), 0) // order
    diagonal = row == lax.broadcasted_iota(jnp.int32, (tile * order, lanes), 1) // width

    @pl.when(pl.program_id(1) == 0)
    def _():
        below = lax.broadcasted_iota(jnp.int32, (SUB, SUB), 0) >= lax.broadcasted_iota(
            jnp.int32, (SUB, SUB), 1
        )
        for g in range(tile):
            wide = jnp.broadcast_to(lags_ref[g : g + 1], (SUB, SUB))
            rolled = pltpu.roll(wide, 0, 1, stride=1, stride_axis=0)
            toep_ref[g * SUB : (g + 1) * SUB] = jnp.where(below, rolled, 0.0).astype(jnp.bfloat16)

    toep = toep_ref[...]
    state = jnp.zeros((tile * order, lanes), jnp.float32)
    for block in range(count // SUB):
        piece = gated[block * SUB : (block + 1) * SUB]
        wide = jnp.dot(toep, piece.astype(jnp.bfloat16), preferred_element_type=jnp.float32)
        local = skip_ref[...] * piece
        picked = wide[:SUB]
        for g in range(1, tile):
            picked = jnp.where(lane == g, wide[g * SUB : (g + 1) * SUB], picked)
        local = local + picked
        if block:
            local = local + product3(reach_ref[:SUB], state)
        base_ref[block * SUB : (block + 1) * SUB] = local
        fresh = product3(leave_ref[...], piece)
        state = fade_ref[...] * state + jnp.where(diagonal, fresh, 0.0)
    compact = state[:order]
    for g in range(1, tile):
        compact = compact + state[g * order : (g + 1) * order]
    state_ref[...] = compact


def convolved(proj, taps, lags, leave, reach, fade, skip, width, order, count):
    chans = skip.shape[1]
    lanes = min(BLOCK, chans)
    steps = chans // lanes
    tile = lanes // width
    _, segments, rows, _ = proj.shape
    return pl.pallas_call(
        functools.partial(conv_kernel, width),
        grid=(steps, segments),
        in_specs=[
            pl.BlockSpec((None, None, rows, lanes), lambda i, j: (i, j, 0, 0)),
            pl.BlockSpec((None, None, rows, lanes), lambda i, j: (i, j, 0, 1)),
            pl.BlockSpec((None, None, rows, lanes), lambda i, j: (i, j, 0, 2)),
            pl.BlockSpec((taps.shape[0], 3, lanes), lambda i, j: (0, 0, i)),
            pl.BlockSpec((tile, SUB), lambda i, j: (i, 0)),
            pl.BlockSpec((tile * order, SUB), lambda i, j: (i, 0)),
            pl.BlockSpec((count, tile * order), lambda i, j: (0, i)),
            pl.BlockSpec((tile * order, 1), lambda i, j: (i, 0)),
            pl.BlockSpec((1, lanes), lambda i, j: (0, i)),
        ],
        out_specs=[
            pl.BlockSpec((None, count, lanes), lambda i, j: (j, 0, i)),
            pl.BlockSpec((None, count, lanes), lambda i, j: (j, 0, i)),
            pl.BlockSpec((None, order, lanes), lambda i, j: (j, 0, i)),
        ],
        out_shape=[
            jax.ShapeDtypeStruct((segments, count, chans), jnp.float32),
            jax.ShapeDtypeStruct((segments, count, chans), jnp.float32),
            jax.ShapeDtypeStruct((segments, order, chans), jnp.float32),
        ],
        scratch_shapes=[pltpu.VMEM((tile * SUB, SUB), jnp.bfloat16)],
        cost_estimate=pl.CostEstimate(
            flops=2 * count * chans * SUB * tile, bytes_accessed=count * chans * 20, transcendentals=0
        ),
        name="conv",
    )(proj, proj, proj, taps, lags, leave, reach, fade, skip)


def place():
    size, here = lax.axis_size("seq"), lax.axis_index("seq")
    return here // 4, lax.rem(here // 2, 2), lax.rem(here, 2), size // 4


def index_of(z, x, core):
    return z * 4 + x * 2 + core


def greet(peers):
    barrier = pltpu.get_barrier_semaphore()
    for peer in peers:
        pl.semaphore_signal(barrier, inc=1, device_id=peer, device_id_type=MESH)
    pl.semaphore_wait(barrier, len(peers))


def remote(source, target, send_sem, recv_sem, peer):
    return pltpu.make_async_remote_copy(
        src_ref=source,
        dst_ref=target,
        send_sem=send_sem,
        recv_sem=recv_sem,
        device_id=peer,
        device_id_type=MESH,
    )


def gather_kernel(
    own_ref, halo_ref, w3_ref, out_ref, proj_ref, wo_ref, tok_ref, w_ref, acc_ref, local_sems, own_sems,
    line_send, line_recv, pass_send, pass_recv, pair_send, pair_recv,
    tp_send, tp_recv, core_send, core_recv, early_send, early_recv,
    cols_send, cols_recv, swap_send, swap_recv, halo_send, halo_recv,
):
    z, x, core, depth = place()
    parity = lax.rem(z, 2)
    n_tp, part = lax.axis_size("tp"), lax.axis_index("tp")
    mine = index_of(z, x, core)
    side = {"seq": index_of(z, 1 - x, core)}
    twin = {"seq": index_of(z, x, 1 - core)}
    blocks, _, _, lanes = w_ref.shape
    rows = w3_ref.shape[1]
    total = blocks * depth

    def on_line(hop):
        there = z ^ hop[0]
        return there, (1 - core if hop[1] else core)

    hops = [(step, other) for step in range(depth) for other in range(2)][1:]
    peers = [side] + [
        {"seq": index_of(there, x, which)} for there, which in map(on_line, hops)
    ]
    tps = [{"tp": lax.rem(part + d, n_tp)} for d in range(1, n_tp)]
    greet(peers + tps)

    cols = own_ref.shape[1] // (2 * n_tp)

    def band(which, piece):
        return pl.ds(pl.multiple_of((2 * which + piece) * cols, cols), cols)

    own_slot, mate_slot = 2 * parity + core, 2 * (1 - parity) + core
    body = pl.ds(HALO, own_ref.shape[0])
    head = pl.ds(0, HALO)
    taken = [
        pltpu.make_async_copy(own_ref, tok_ref.at[own_slot, body], local_sems.at[0]),
        pltpu.make_async_copy(halo_ref, tok_ref.at[own_slot, head], local_sems.at[1]),
    ]
    started = []

    def begin(*what):
        copy = remote(*what)
        copy.start()
        started.append(copy)
        return copy

    def wide(role, block):
        return w3_ref.at[:, :, pl.ds(pl.multiple_of((role * blocks + block) * lanes, lanes), lanes)]

    def landed(block, source):
        return w_ref.at[block, :, pl.ds(pl.multiple_of(source * rows, rows), rows), :]

    def own_piece(block):
        return pltpu.make_async_copy(wide(own_slot, block), landed(block, mine), own_sems.at[block])

    def first(block):
        return remote(
            wide(own_slot, block), landed(block, mine),
            pass_send.at[block, 0], pass_recv.at[block, 0], side,
        )

    def line(block, hop):
        there, which = on_line(hop)
        index = 2 * hop[0] + hop[1]
        return remote(
            wide(2 * lax.rem(there, 2) + which, block), landed(block, mine),
            line_send.at[block, index], line_recv.at[block, index], {"seq": index_of(there, x, which)},
        )

    def arriving(block, hop):
        there, which = on_line(hop)
        index = 2 * hop[0] + hop[1]
        where = landed(block, index_of(there, x, which))
        return remote(
            where, where, line_send.at[block, index], line_recv.at[block, index],
            {"seq": index_of(there, x, which)},
        )

    def passing(block, hop):
        there, which = on_line(hop)
        index = 2 * hop[0] + hop[1]
        where = landed(block, index_of(there, x, which))
        return remote(where, where, pass_send.at[block, index], pass_recv.at[block, index], side)

    def passed(block, hop):
        there, which = on_line(hop)
        index = 2 * hop[0] + hop[1]
        where = landed(block, index_of(there, 1 - x, which))
        return remote(where, where, pass_send.at[block, index], pass_recv.at[block, index], side)

    def to_pair(piece):
        where = tok_ref.at[own_slot, body, band(part, piece)]
        return begin(
            own_ref.at[:, band(part, piece)], where, pair_send.at[piece], pair_recv.at[piece],
            {"seq": index_of(z ^ 1, x, core)},
        )

    quarter = wo_ref.shape[1] // 4
    out_cols = wo_ref.shape[2]

    def quarter_rows(piece):
        return pl.ds(pl.multiple_of((2 * core + piece) * quarter, quarter), quarter)

    def columns(d, piece):
        target = lax.rem(part + d, n_tp)
        slot = 2 * (d - 1) + piece
        return begin(
            out_ref.at[quarter_rows(piece), pl.ds(pl.multiple_of(target * out_cols, out_cols), out_cols)],
            wo_ref.at[d - 1, quarter_rows(piece)],
            cols_send.at[slot], cols_recv.at[slot], tps[d - 1],
        )

    def swap(d, piece):
        slot = 2 * (d - 1) + piece
        where = wo_ref.at[d - 1, quarter_rows(piece)]
        return begin(where, where, swap_send.at[slot], swap_recv.at[slot], twin)

    for copy in taken:
        copy.start()

    def issue(block):
        own_piece(block).start()
        first(block).start()
        for hop in hops:
            line(block, hop).start()

    paired = [to_pair(0)]
    own_piece(0).start()
    first(0).start()
    for hop in hops[:3]:
        line(0, hop).start()
    paired.append(to_pair(1))
    for hop in hops[3:]:
        line(0, hop).start()
    moved = {(d, 0): columns(d, 0) for d in range(1, n_tp)}
    early = begin(own_ref, tok_ref.at[own_slot, body], early_send, early_recv, twin)
    heads = []
    for n, hop in enumerate(hops[:3]):
        there, which = on_line(hop)
        heads.append(begin(
            halo_ref, tok_ref.at[own_slot, head], halo_send.at[n], halo_recv.at[n],
            {"seq": index_of(there, x, which)},
        ))

    def forward(n):
        block, step = n // depth, lax.rem(n, depth)

        @pl.when(step > 0)
        def _():
            arriving(block, (step, 0)).wait_recv()
            passing(block, (step, 0)).start()

        arriving(block, (step, 1)).wait_recv()
        passing(block, (step, 1)).start()

    twins, across = [], {}

    def to_twin(which, piece, d):
        where = tok_ref.at[mate_slot, body, band(which, piece)]
        slot = 2 * d + piece
        twins.append(begin(where, where, core_send.at[slot], core_recv.at[slot], twin))

    def pair_on(piece):
        paired[piece].wait_recv()
        where = tok_ref.at[mate_slot, body, band(part, piece)]
        for d in range(1, n_tp):
            slot = 2 * (d - 1) + piece
            across[d, piece] = begin(
                where, where, tp_send.at[slot], tp_recv.at[slot], tps[d - 1]
            )
        to_twin(part, piece, 0)

    forward(0)
    pair_on(0)
    forward(1)
    pair_on(1)
    for d in range(1, n_tp):
        moved[d, 1] = columns(d, 1)
    if blocks > 1:
        issue(1)
    for n in range(2, depth):
        forward(n)
    for piece in range(2):
        for d in range(1, n_tp):
            across[d, piece].wait_recv()
            to_twin(lax.rem(part - d + n_tp, n_tp), piece, d)
    for copy in taken:
        copy.wait()
    for copy in [early] + heads + twins:
        copy.wait_recv()

    depth_rows = 4 * rows

    def compute(n):
        block, step = n // depth, lax.rem(n, depth)

        @pl.when(step == 0)
        def _():
            own_piece(block).wait()

        for other in range(2):
            passed(block, (step, other)).wait_recv()
        span = pl.ds(pl.multiple_of((z ^ step) * depth_rows, depth_rows), depth_rows)

        def one(slot, carry):
            right = jnp.concatenate([w_ref[block, p, span, :] for p in range(3)], axis=1)
            value = jnp.dot(tok_ref[slot, :, span], right, preferred_element_type=jnp.float32)

            @pl.when(step == 0)
            def _():
                acc_ref[slot] = value

            @pl.when(step > 0)
            def _():
                acc_ref[slot] = acc_ref[slot] + value

            return carry

        lax.fori_loop(0, 4, one, 0)

        @pl.when(step == depth - 1)
        def _():
            def put(slot, carry):
                for p in range(3):
                    proj_ref[block, slot, :, p * lanes : (p + 1) * lanes] = acc_ref[
                        slot, :, p * lanes : (p + 1) * lanes
                    ].astype(proj_ref.dtype)
                return carry

            lax.fori_loop(0, 4, put, 0)

    lag = min(2, depth)

    def early_step(n, carry):
        compute(n)
        return carry

    lax.fori_loop(0, depth - lag, early_step, 0)

    def step(n, carry):
        block = n // depth

        @pl.when((lax.rem(n, depth) == 0) & (block + 1 < blocks))
        def _():
            issue(block + 1)

        forward(n)
        compute(n - lag)
        return carry

    lax.fori_loop(depth, total, step, 0)
    for piece in range(2):
        for d in range(1, n_tp):
            moved[d, piece].wait_recv()
            twins_swap = swap(d, piece)
            heads.append(twins_swap)
    lax.fori_loop(total - lag, total, early_step, 0)
    for copy in heads[3:]:
        copy.wait_recv()
    for copy in started:
        copy.wait_send()

    def finish(block, carry):
        first(block).wait_send()
        for hop in hops:
            line(block, hop).wait_send()
            passing(block, hop).wait_send()
        return carry

    lax.fori_loop(0, blocks, finish, 0)


def gathered(own, halo, w3, w_out):
    size, n_tp = lax.axis_size("seq"), lax.axis_size("tp")
    line = size // 2
    chans = w3.shape[2] // 4
    lanes = min(BLOCK, chans)
    blocks = chans // lanes
    tall = HALO + own.shape[0]
    anywhere = pl.BlockSpec(memory_space=pl.ANY)
    counts = [3, blocks] + [(blocks, line)] * 4 + [2, 2] + [2 * n_tp] * 4 + [0, 0] + [2 * n_tp] * 4 + [3, 3]
    return pl.pallas_call(
        gather_kernel,
        out_shape=[
            jax.ShapeDtypeStruct((blocks, 4, tall, 3 * lanes), own.dtype),
            jax.ShapeDtypeStruct(
                (n_tp - 1, w_out.shape[0], w_out.shape[1] // n_tp), w_out.dtype
            ),
        ],
        in_specs=[anywhere] * 4,
        out_specs=[pl.BlockSpec(memory_space=pltpu.VMEM), anywhere],
        scratch_shapes=[
            pltpu.VMEM((4, tall, own.shape[1]), own.dtype),
            pltpu.VMEM((blocks, 3, own.shape[1], lanes), w3.dtype),
            pltpu.VMEM((4, tall, 3 * lanes), jnp.float32),
        ]
        + [pltpu.SemaphoreType.DMA(n if isinstance(n, tuple) else (n,) if n else ()) for n in counts],
        compiler_params=pltpu.CompilerParams(
            collective_id=0, has_side_effects=True, vmem_limit_bytes=60 << 20
        ),
        name="gather",
    )(own, halo, w3, w_out)


def share_kernel(own_ref, all_ref, send_sems, recv_sems):
    total = all_ref.shape[0]
    z, x, core, depth = place()
    here = (z // 2) * 2 + x

    def peer(d):
        there = lax.rem(here + d, total)
        return {"seq": index_of(2 * (there // 2) + lax.rem(z, 2), lax.rem(there, 2), core)}

    peers = [peer(d) for d in range(1, total)]
    greet(peers)
    copies = []
    for d in range(1, total):
        copy = remote(
            own_ref, all_ref.at[here], send_sems.at[d - 1], recv_sems.at[d - 1], peers[d - 1]
        )
        copy.start()
        copies.append(copy)
    all_ref[here] = own_ref[...]
    for copy in copies:
        copy.wait()


def shared(state):
    total = lax.axis_size("seq") // 4
    return pl.pallas_call(
        share_kernel,
        out_shape=jax.ShapeDtypeStruct((total,) + state.shape, state.dtype),
        in_specs=[pl.BlockSpec(memory_space=pltpu.VMEM)],
        out_specs=pl.BlockSpec(memory_space=pltpu.VMEM),
        scratch_shapes=[
            pltpu.SemaphoreType.DMA((total - 1,)),
            pltpu.SemaphoreType.DMA((total - 1,)),
        ],
        compiler_params=pltpu.CompilerParams(collective_id=1, has_side_effects=True),
        name="share",
    )(state)


def spread_kernel(mix_ref, full_ref, local_sem, send_sems, recv_sems, tp_send, tp_recv):
    z, x, core, _ = place()
    chans = mix_ref.shape[2]
    n_tp, part = lax.axis_size("tp"), lax.axis_index("tp")
    parity = lax.rem(z, 2)
    me = 2 * parity + core

    def peer(d):
        there = (z ^ (d // 2), (1 - core if d % 2 else core))
        return 2 * lax.rem(there[0], 2) + there[1], {"seq": index_of(there[0], x, there[1])}

    tps = [{"tp": lax.rem(part + d, n_tp)} for d in range(1, n_tp)]
    greet([peer(d)[1] for d in range(1, 4)] + tps)

    def at(slot, which):
        return full_ref.at[slot, :, pl.ds(pl.multiple_of(which * chans, chans), chans)]

    across = []

    def over(source, which, n):
        for d in range(1, n_tp):
            sem = 4 * (d - 1) + n
            copy = remote(source, at(d, which), tp_send.at[sem], tp_recv.at[sem], tps[d - 1])
            copy.start()
            across.append(copy)

    copies = []
    for d in (2, 3, 1):
        there, device = peer(d)
        copy = remote(
            mix_ref.at[there], at(0, me), send_sems.at[d - 1], recv_sems.at[d - 1], device
        )
        copy.start()
        copies.append((d, copy))
    over(mix_ref.at[me], me, 0)
    stay = pltpu.make_async_copy(mix_ref.at[me], at(0, me), local_sem)
    stay.start()
    for d, copy in copies[2:] + copies[:2]:
        copy.wait_recv()
        which = peer(d)[0]
        over(at(0, which), which, d)
    for _, copy in copies:
        copy.wait_send()
    for copy in across:
        copy.wait()
    stay.wait()


def spread(mix):
    n_tp = lax.axis_size("tp")
    roles, count, chans = mix.shape
    return pl.pallas_call(
        spread_kernel,
        out_shape=jax.ShapeDtypeStruct((n_tp, count, roles * chans), mix.dtype),
        in_specs=[pl.BlockSpec(memory_space=pltpu.VMEM)],
        out_specs=pl.BlockSpec(memory_space=pltpu.VMEM),
        scratch_shapes=[
            pltpu.SemaphoreType.DMA(()),
            pltpu.SemaphoreType.DMA((3,)),
            pltpu.SemaphoreType.DMA((3,)),
            pltpu.SemaphoreType.DMA((4 * n_tp,)),
            pltpu.SemaphoreType.DMA((4 * n_tp,)),
        ],
        compiler_params=pltpu.CompilerParams(collective_id=2, has_side_effects=True),
        name="spread",
    )(mix)


def mix_kernel(width, query_ref, base_ref, all_ref, weight_ref, reach_ref, mix_ref):
    order = all_ref.shape[1]
    entering = jnp.sum(all_ref[...] * weight_ref[...], axis=0)
    carried = product3(reach_ref[...], fanned(entering, width, order))
    mix_ref[...] = (query_ref[...] * (base_ref[...] + carried)).astype(mix_ref.dtype)


def mixed_of(query, base, everything, weight, reach, width):
    segments, count, chans = query.shape
    size, order, _ = everything.shape
    lanes = min(LANES, chans)
    cols = lanes // width * order
    return pl.pallas_call(
        functools.partial(mix_kernel, width),
        grid=(chans // lanes, segments),
        in_specs=[
            pl.BlockSpec((None, count, lanes), lambda i, j: (j, 0, i)),
            pl.BlockSpec((None, count, lanes), lambda i, j: (j, 0, i)),
            pl.BlockSpec((size, order, lanes), lambda i, j: (0, 0, i)),
            pl.BlockSpec((None, size, order, lanes), lambda i, j: (j, 0, 0, i)),
            pl.BlockSpec((count, cols), lambda i, j: (0, i)),
        ],
        out_specs=pl.BlockSpec((None, count, lanes), lambda i, j: (j, 0, i)),
        out_shape=jax.ShapeDtypeStruct((segments, count, chans), jnp.bfloat16),
        name="mix",
    )(query, base, everything, weight, reach)


def shards(tokens, w_in, short_taps, decay_rate, residue, skip_gain, w_out):
    count = tokens.shape[0]
    all_chans = w_in.shape[2]
    width = all_chans // decay_rate.shape[0]
    taps = short_taps.shape[0]
    z, x, core, depth = place()
    parity = lax.rem(z, 2)
    role = 2 * parity + core
    n_tp, part = lax.axis_size("tp"), lax.axis_index("tp")
    chans = all_chans // 4

    before = shifted_by(tokens[count - (taps - 1) :], "seq", 1)
    halo = jnp.pad(before, ((HALO - (taps - 1), 0), (0, 0)))
    proj, out_rows = gathered(tokens, halo, w_in.transpose(1, 0, 2), w_out)

    def own(array, axis):
        share = array.shape[axis] // 4
        return lax.dynamic_slice_in_dim(array, role * share, share, axis)

    short_taps, skip = own(short_taps, 2), own(skip_gain[None], 1)
    decay_rate, residue = own(decay_rate, 0), own(residue, 0)
    groups, order = decay_rate.shape
    weight_mode = residue * jnp.sqrt(2.0 * decay_rate / order)
    offsets = jnp.arange(SUB, dtype=jnp.float32)
    back = (-jnp.arange(SUB) % SUB).astype(jnp.float32)
    lags = jnp.einsum(
        "gm,gmd->gd",
        weight_mode,
        jnp.exp(-decay_rate[:, :, None] * back[None, None, :]),
        precision=HIGHEST,
    )
    rate = decay_rate.reshape(groups * order)
    leave = jnp.exp(-rate[:, None] * (SUB - 1.0 - offsets[None, :]))
    fade = jnp.exp(-rate * SUB)[:, None]
    positions = jnp.arange(count, dtype=jnp.float32)
    reach = weight_mode.reshape(groups * order)[None] * jnp.exp(
        -rate[None] * (positions[:, None] + 1.0)
    )
    by_mode = jnp.repeat(decay_rate.T, width, axis=1)
    slot = jnp.arange(4)
    own_block = index_of(2 * (z // 2) + slot // 2, x, slot % 2)
    team = jnp.arange(depth)[:, None]
    other_block = index_of(2 * (team // 2) + slot[None] // 2, team % 2, slot[None] % 2).reshape(-1)
    ahead = (own_block[:, None] - 1 - other_block[None, :])[:, :, None, None]
    weight = jnp.where(
        ahead >= 0, jnp.exp(-by_mode * (count * jnp.maximum(ahead, 0).astype(jnp.float32))), 0.0
    )

    query, base, final = convolved(
        proj, short_taps, lags, leave, reach, fade, skip, width, order, count
    )
    everything = shared(final).reshape(-1, order, chans)
    full = spread(mixed_of(query, base, everything, weight, reach, width))

    share = w_out.shape[1] // n_tp
    kept = lax.dynamic_slice_in_dim(w_out, part * share, share, axis=1)
    total = jnp.dot(full[0], kept, preferred_element_type=jnp.float32)
    for d in range(1, n_tp):
        total = total + jnp.dot(full[d], out_rows[d - 1], preferred_element_type=jnp.float32)
    return total.astype(jnp.bfloat16)


def solution(mesh):
    in_specs = (
        P("seq", None),
        P("seq", None, "tp"),
        P(None, None, "tp"),
        P("tp", None),
        P("tp", None),
        P("tp"),
        P("tp", None),
    )
    out_specs = P("seq", "tp")
    return jax.shard_map(shards, mesh=mesh, in_specs=in_specs, out_specs=out_specs, check_vma=False)
```

```python
import functools

import jax
import jax.numpy as jnp
from jax import lax
from jax.experimental import pallas as pl
from jax.experimental.pallas import tpu as pltpu
from jax.sharding import PartitionSpec as P

SUB = 128
BLOCK = 128
COLUMN_PIECES = 8
HALO = 16
MESH = pl.DeviceIdType.MESH
HIGHEST = lax.Precision.HIGHEST


def shifted_by(block, axis, distance):
    devices = range(lax.axis_size(axis))
    route = [(i - distance, i) for i in devices if i - distance in devices]
    return lax.ppermute(block, axis, route)


def fanned(state, width, order):
    lanes = state.shape[1]
    tile = lanes // width
    full = jnp.concatenate([state] * tile, axis=0)
    row = lax.broadcasted_iota(jnp.int32, full.shape, 0) // order
    lane = lax.broadcasted_iota(jnp.int32, full.shape, 1) // width
    return jnp.where(row == lane, full, 0.0)


def split(value):
    high = value.astype(jnp.bfloat16)
    return high, (value - high.astype(jnp.float32)).astype(jnp.bfloat16)


def product_split(a, b):
    (ah, al), (bh, bl) = a, b
    dot = functools.partial(jnp.dot, preferred_element_type=jnp.float32)
    return dot(ah, bh) + (dot(ah, bl) + dot(al, bh))


def place():
    size, here = lax.axis_size("seq"), lax.axis_index("seq")
    return here // 4, lax.rem(here // 2, 2), lax.rem(here, 2), size // 4


def index_of(z, x, core):
    return z * 4 + x * 2 + core


def greet(peers):
    barrier = pltpu.get_barrier_semaphore()
    for peer in peers:
        pl.semaphore_signal(barrier, inc=1, device_id=peer, device_id_type=MESH)
    pl.semaphore_wait(barrier, len(peers))


def remote(source, target, send_sem, recv_sem, peer):
    return pltpu.make_async_remote_copy(
        src_ref=source,
        dst_ref=target,
        send_sem=send_sem,
        recv_sem=recv_sem,
        device_id=peer,
        device_id_type=MESH,
    )


def hyena_kernel(
    width,
    own_ref, w3_ref, out_ref, taps_ref, lags_ref, leave_ref, reach_ref, fade_ref, skip_ref, mode_ref,
    mixed_ref, wo_ref,
    tok_ref, w_ref, acc_ref, proj_ref, toep_ref, query_ref, base_ref, all_ref, mix_ref, full_ref, total_ref,
    local_sems, own_sems,
    line_send, line_recv, pass_send, pass_recv, pair_send, pair_recv,
    tp_send, tp_recv, core_send, core_recv, early_send, early_recv,
    cols_send, cols_recv, swap_send, swap_recv, halo_send, halo_recv,
    share_send, share_recv, role_send, role_recv, over_send, over_recv,
):
    z, x, core, depth = place()
    parity = lax.rem(z, 2)
    n_tp, part = lax.axis_size("tp"), lax.axis_index("tp")
    size = lax.axis_size("seq")
    mine = index_of(z, x, core)
    side = {"seq": index_of(z, 1 - x, core)}
    twin = {"seq": index_of(z, x, 1 - core)}
    blocks, _, _, lanes = w_ref.shape
    rows = w3_ref.shape[1]
    count = own_ref.shape[0]
    taps = taps_ref.shape[0]
    order = all_ref.shape[3]
    tile = lanes // width
    modes = tile * order
    total = blocks * depth

    def on_line(hop):
        there = z ^ hop[0]
        return there, (1 - core if hop[1] else core)

    hops = [(step, other) for step in range(depth) for other in range(2)][1:]
    tps = [{"tp": lax.rem(part + d, n_tp)} for d in range(1, n_tp)]
    greet([{"seq": lax.rem(mine + d, size)} for d in range(1, size)] + tps)

    cols = own_ref.shape[1] // (2 * n_tp)

    def band(which, piece):
        return pl.ds(pl.multiple_of((2 * which + piece) * cols, cols), cols)

    own_slot, mate_slot = 2 * parity + core, 2 * (1 - parity) + core
    body = pl.ds(HALO, count)
    edge = pl.ds(HALO // 2, HALO // 2)
    taken = pltpu.make_async_copy(own_ref, tok_ref.at[own_slot, body], local_sems.at[0])
    started = []

    def begin(*what):
        copy = remote(*what)
        copy.start()
        started.append(copy)
        return copy

    def wide(role, block):
        return w3_ref.at[:, :, pl.ds(pl.multiple_of((role * blocks + block) * lanes, lanes), lanes)]

    def landed(block, source):
        return w_ref.at[block, :, pl.ds(pl.multiple_of(source * rows, rows), rows), :]

    def own_piece(block):
        return pltpu.make_async_copy(wide(own_slot, block), landed(block, mine), own_sems.at[block])

    def first(block):
        return remote(
            wide(own_slot, block), landed(block, mine),
            pass_send.at[block, 0], pass_recv.at[block, 0], side,
        )

    def line(block, hop):
        there, which = on_line(hop)
        index = 2 * hop[0] + hop[1]
        return remote(
            wide(2 * lax.rem(there, 2) + which, block), landed(block, mine),
            line_send.at[block, index], line_recv.at[block, index], {"seq": index_of(there, x, which)},
        )

    def arriving(block, hop):
        there, which = on_line(hop)
        index = 2 * hop[0] + hop[1]
        where = landed(block, index_of(there, x, which))
        return remote(
            where, where, line_send.at[block, index], line_recv.at[block, index],
            {"seq": index_of(there, x, which)},
        )

    def passing(block, hop):
        there, which = on_line(hop)
        index = 2 * hop[0] + hop[1]
        where = landed(block, index_of(there, x, which))
        return remote(where, where, pass_send.at[block, index], pass_recv.at[block, index], side)

    def passed(block, hop):
        there, which = on_line(hop)
        index = 2 * hop[0] + hop[1]
        where = landed(block, index_of(there, 1 - x, which))
        return remote(where, where, pass_send.at[block, index], pass_recv.at[block, index], side)

    def to_pair(piece):
        where = tok_ref.at[own_slot, body, band(part, piece)]
        return begin(
            own_ref.at[:, band(part, piece)], where, pair_send.at[piece], pair_recv.at[piece],
            {"seq": index_of(z ^ 1, x, core)},
        )

    portion = wo_ref.shape[1] // (2 * COLUMN_PIECES)
    out_cols = wo_ref.shape[2]

    def portion_rows(piece):
        return pl.ds(pl.multiple_of((COLUMN_PIECES * core + piece) * portion, portion), portion)

    def out_span(which):
        return pl.ds(pl.multiple_of(which * out_cols, out_cols), out_cols)

    moved = {}

    def columns(pieces):
        for piece in pieces:
            for d in range(1, n_tp):
                slot = COLUMN_PIECES * (d - 1) + piece
                moved[d, piece] = begin(
                    out_ref.at[portion_rows(piece), out_span(lax.rem(part + d, n_tp))],
                    wo_ref.at[d - 1, portion_rows(piece)],
                    cols_send.at[slot], cols_recv.at[slot], tps[d - 1],
                )

    def swap(d, piece):
        slot = COLUMN_PIECES * (d - 1) + piece
        where = wo_ref.at[d - 1, portion_rows(piece)]
        return begin(where, where, swap_send.at[slot], swap_recv.at[slot], twin)

    after = jnp.where(x == 0, z, z + 1)
    leads = (core == 1) & ((x == 0) | (z < depth - 1))

    def edges():
        copies = []
        for n in range(4):
            slot = 2 * lax.rem(after, 2)
            copies.append(remote(
                own_ref.at[pl.ds(count - HALO // 2, HALO // 2)], tok_ref.at[slot, edge],
                halo_send.at[n], halo_recv.at[lax.rem(after, 2)],
                {"seq": index_of(after ^ (n // 2), 1 - x, n % 2)},
            ))
        return copies

    inner = (lax.rem(z, 4) == 1) | (lax.rem(z, 4) == 2)

    def step_of(n):
        turn = lax.rem(n, depth)
        rolled = lax.rem(turn + depth - 3, depth - 1) + 1
        return jnp.where(inner & (turn > 0), rolled, turn)

    def forward(n):
        block, step = n // depth, step_of(n)
        for other in range(2):
            arriving(block, (step, other)).wait_recv()
            passing(block, (step, other)).start()

    def forward_ahead(block, carry):
        forward(block * depth + 1)
        return carry

    def near(block, carry):
        arriving(block, (0, 1)).wait_recv()
        passing(block, (0, 1)).start()
        return carry

    def begin_own(block, carry):
        own_piece(block).start()
        first(block).start()
        line(block, (0, 1)).start()
        return carry

    def issue_step(block, step):
        for other in range(2):
            line(block, (step, other)).start()

    def issue(block):
        @pl.when(jnp.logical_not(inner))
        def _():
            issue_step(block, depth - 1)

        for step in range(1, depth - 1):
            issue_step(block, step)

    def issue_ahead(block, carry):
        issue_step(block, depth - 1)
        return carry

    taken.start()
    columns(range(2))
    paired = [to_pair(0), to_pair(1)]
    lax.fori_loop(0, blocks, begin_own, 0)

    @pl.when(leads)
    def _():
        for copy in edges():
            copy.start()

    @pl.when(inner)
    def _():
        lax.fori_loop(0, blocks, issue_ahead, 0)

    issue(0)
    early = begin(own_ref, tok_ref.at[own_slot, body], early_send, early_recv, twin)
    twins, across = [], {}

    def to_twin(which, piece, d):
        where = tok_ref.at[mate_slot, body, band(which, piece)]
        slot = 2 * d + piece
        twins.append(begin(where, where, core_send.at[slot], core_recv.at[slot], twin))

    def pair_on(piece):
        paired[piece].wait_recv()
        where = tok_ref.at[mate_slot, body, band(part, piece)]
        for d in range(1, n_tp):
            slot = 2 * (d - 1) + piece
            across[d, piece] = begin(
                where, where, tp_send.at[slot], tp_recv.at[slot], tps[d - 1]
            )
        to_twin(part, piece, 0)

    lax.fori_loop(0, blocks, near, 0)
    if blocks > 1:
        issue(1)
    half = blocks // 2

    @pl.when(inner)
    def _():
        lax.fori_loop(0, half, forward_ahead, 0)

    pair_on(0)
    columns(range(2, 3))

    @pl.when(inner)
    def _():
        lax.fori_loop(half, blocks, forward_ahead, 0)

    pair_on(1)
    columns(range(3, COLUMN_PIECES))

    @pl.when(jnp.logical_not(inner))
    def _():
        forward(1)

    for n in range(2, depth):
        forward(n)
    for piece in range(2):
        for d in range(1, n_tp):
            across[d, piece].wait_recv()
            to_twin(lax.rem(part - d + n_tp, n_tp), piece, d)
    taken.wait()
    for copy in [early] + twins:
        copy.wait_recv()
    for p in range(2):
        starts = (z - parity + p == 0) & (x == 0)

        @pl.when(starts)
        def _():
            tok_ref[2 * p, HALO // 2 : HALO] = jnp.zeros(
                (HALO // 2, tok_ref.shape[2]), tok_ref.dtype
            )

        @pl.when(jnp.logical_not(starts))
        def _():
            where = tok_ref.at[2 * p, edge]
            remote(where, where, halo_send.at[0], halo_recv.at[p], side).wait_recv()

        tok_ref[2 * p + 1, HALO // 2 : HALO] = tok_ref[2 * p, HALO // 2 + count : HALO + count]

    depth_rows = 4 * rows

    def compute(n):
        block, step = n // depth, step_of(n)

        @pl.when(step == 0)
        def _():
            own_piece(block).wait()

        for other in range(2):
            passed(block, (step, other)).wait_recv()
        span = pl.ds(pl.multiple_of((z ^ step) * depth_rows, depth_rows), depth_rows)

        def one(slot, carry):
            right = jnp.concatenate([w_ref[block, p, span, :] for p in range(3)], axis=1)
            value = jnp.dot(tok_ref[slot, :, span], right, preferred_element_type=jnp.float32)

            @pl.when(step == 0)
            def _():
                acc_ref[slot] = value

            @pl.when(step != 0)
            def _():
                acc_ref[slot] = acc_ref[slot] + value

            return carry

        lax.fori_loop(0, 4, one, 0)

        @pl.when(lax.rem(n, depth) == depth - 1)
        def _():
            def put(slot, carry):
                proj_ref[slot] = acc_ref[slot].astype(proj_ref.dtype)
                return carry

            lax.fori_loop(0, 4, put, 0)

    team = (z // 2) * 2 + x
    lane = lax.broadcasted_iota(jnp.int32, (SUB, 2 * lanes), 1)
    lane = lax.rem(lane, lanes) // width
    diagonal = (
        lax.broadcasted_iota(jnp.int32, (modes, lanes), 0) // order
        == lax.broadcasted_iota(jnp.int32, (modes, lanes), 1) // width
    )

    def chan(block):
        return pl.ds(pl.multiple_of((own_slot * blocks + block) * lanes, lanes), lanes)

    def convolve(block):
        below = lax.broadcasted_iota(jnp.int32, (SUB, SUB), 0) >= lax.broadcasted_iota(
            jnp.int32, (SUB, SUB), 1
        )
        lags = lags_ref[pl.ds(pl.multiple_of(block * tile, tile), tile)]
        for g in range(tile):
            turned = pltpu.roll(
                jnp.broadcast_to(lags[g : g + 1], (SUB, SUB)), 0, 1, stride=1, stride_axis=0
            )
            toep_ref[g * SUB : (g + 1) * SUB] = jnp.where(below, turned, 0.0).astype(jnp.bfloat16)
        span = pl.ds(pl.multiple_of(block * modes, modes), modes)
        leave = split(leave_ref[span])
        reach = split(reach_ref[block, :SUB])
        fade = fade_ref[span]
        skip = skip_ref[:, chan(block)]
        skip = jnp.concatenate([skip, skip], axis=1)
        kernel_taps = [[taps_ref[tap, w : w + 1, chan(block)] for w in range(3)] for tap in range(taps)]

        def segment(slot, carry):
            def filtered(which):
                value = proj_ref[slot, :, which * lanes : (which + 1) * lanes].astype(jnp.float32)
                out = None
                for tap in range(taps):
                    term = kernel_taps[tap][which] * value[HALO - tap : HALO - tap + count]
                    out = term if out is None else out + term
                return out

            query_ref[slot] = filtered(0)
            gated = filtered(1) * filtered(2)
            state = jnp.zeros((modes, lanes), jnp.float32)
            for two in range(count // SUB // 2):
                low, high = 2 * two * SUB, (2 * two + 1) * SUB
                piece = jnp.concatenate([gated[low:high], gated[high : high + SUB]], axis=1)
                spread = jnp.dot(
                    toep_ref[...], piece.astype(jnp.bfloat16), preferred_element_type=jnp.float32
                )
                picked = spread[:SUB]
                for g in range(1, tile):
                    picked = jnp.where(lane == g, spread[g * SUB : (g + 1) * SUB], picked)
                local = skip * piece + picked
                fresh = product_split(leave, split(piece))
                for turn, start in ((0, low), (1, high)):
                    value = local[:, turn * lanes : (turn + 1) * lanes]
                    if start:
                        value = value + product_split(reach, split(state))
                    base_ref[slot, start : start + SUB] = value
                    state = fade * state + jnp.where(
                        diagonal, fresh[:, turn * lanes : (turn + 1) * lanes], 0.0
                    )
            compact = state[:order]
            for g in range(1, tile):
                compact = compact + state[g * order : (g + 1) * order]
            all_ref[block, team, slot] = compact
            return carry

        lax.fori_loop(0, 4, segment, 0)

    def teammate(d):
        there = lax.rem(team + d, depth)
        return there, {
            "seq": index_of(2 * (there // 2) + parity, lax.rem(there, 2), core)
        }

    def shares(block):
        return [
            remote(
                all_ref.at[block, team], all_ref.at[block, team],
                share_send.at[block, d - 1], share_recv.at[block, d - 1], teammate(d)[1],
            )
            for d in range(1, depth)
        ]

    def share_waits(block):
        return [
            remote(
                all_ref.at[block, lax.rem(team - d + depth, depth)],
                all_ref.at[block, lax.rem(team - d + depth, depth)],
                share_send.at[block, d - 1], share_recv.at[block, d - 1], teammate(d)[1],
            )
            for d in range(1, depth)
        ]

    def colleague(d):
        there, which = z ^ (d // 2), (1 - core if d % 2 else core)
        return 2 * lax.rem(there, 2) + which, {"seq": index_of(there, x, which)}

    def combine(block):
        for copy in share_waits(block):
            copy.wait_recv()
        rates = mode_ref[:, chan(block)]
        reach = split(reach_ref[block])

        def segment(slot, carry):
            here = index_of(z - parity + slot // 2, x, lax.rem(slot, 2))

            def member(n, entering):
                for other in range(4):
                    ahead = here - 1 - index_of(
                        2 * (n // 2) + other // 2, lax.rem(n, 2), other % 2
                    )
                    far = (count * jnp.maximum(ahead, 0)).astype(jnp.float32)
                    weight = jnp.where(ahead >= 0, jnp.exp(-rates * far), 0.0)
                    entering = entering + weight * all_ref[block, n, other]
                return entering

            entering = lax.fori_loop(0, depth, member, jnp.zeros((order, lanes), jnp.float32))
            carried = product_split(reach, split(fanned(entering, width, order)))
            mix_ref[block, slot] = (query_ref[slot] * (base_ref[slot] + carried)).astype(mix_ref.dtype)
            return carry

        lax.fori_loop(0, 4, segment, 0)
        full_ref[0, block, own_slot] = mix_ref[block, own_slot]

    def roles(block):
        return [
            remote(
                mix_ref.at[block, colleague(d)[0]], full_ref.at[0, block, own_slot],
                role_send.at[block, d - 1], role_recv.at[block, d - 1], colleague(d)[1],
            )
            for d in (2, 3, 1)
        ]

    def role_waits(block):
        return [
            remote(
                full_ref.at[0, block, colleague(d)[0]], full_ref.at[0, block, colleague(d)[0]],
                role_send.at[block, d - 1], role_recv.at[block, d - 1], colleague(d)[1],
            )
            for d in range(1, 4)
        ]

    def overs(block, n):
        which = colleague(n)[0]
        return [
            remote(
                full_ref.at[0, block, which], full_ref.at[d, block, which],
                over_send.at[block, 4 * (d - 1) + n], over_recv.at[block, 4 * (d - 1) + n], tps[d - 1],
            )
            for d in range(1, n_tp)
        ]

    def over_waits(block):
        return [
            remote(
                full_ref.at[d, block, colleague(n)[0]], full_ref.at[d, block, colleague(n)[0]],
                over_send.at[block, 4 * (d - 1) + n], over_recv.at[block, 4 * (d - 1) + n], tps[d - 1],
            )
            for n in range(4)
            for d in range(1, n_tp)
        ]

    def send_states(block):
        for copy in shares(block):
            copy.start()

    def send_mix(block):
        for copy in roles(block) + overs(block, 0):
            copy.start()

    def send_over(block):
        for n, copy in enumerate(role_waits(block)):
            copy.wait_recv()
            for across_copy in overs(block, n + 1):
                across_copy.start()

    lag = 2

    def late_step(n, carry):
        compute(n)
        return carry

    lax.fori_loop(0, depth - lag, late_step, 0)

    def step(n, carry):
        block, turn = n // depth, lax.rem(n, depth)

        @pl.when((turn == 0) & (block + 1 < blocks))
        def _():
            issue(block + 1)

        @pl.when((turn > 1) | ((turn == 1) & jnp.logical_not(inner)))
        def _():
            forward(n)

        compute(n - lag)

        @pl.when(turn == 1)
        def _():
            convolve(block - 1)
            send_states(block - 1)

        @pl.when(turn == 2)
        def _():
            combine(block - 1)
            send_mix(block - 1)

        @pl.when(turn == 3)
        def _():
            send_over(block - 1)

        return carry

    lax.fori_loop(depth, total, step, 0)
    lax.fori_loop(total - lag, total, late_step, 0)
    loads = []

    def load(source, slot, d):
        chans = blocks * lanes
        copy = pltpu.make_async_copy(
            source, tok_ref.at[slot, pl.ds(0, chans), pl.ds(d * out_cols, out_cols)],
            local_sems.at[1 + 4 * d + slot],
        )
        copy.start()
        loads.append(copy)

    def role_rows(slot):
        return pl.ds(slot * blocks * lanes, blocks * lanes)

    inside = twins + list(across.values())
    for copy in inside:
        copy.wait_send()
    for slot in range(4):
        load(out_ref.at[role_rows(slot), out_span(part)], slot, 0)
    convolve(blocks - 1)
    send_states(blocks - 1)
    combine(blocks - 1)
    send_mix(blocks - 1)
    swaps = []
    for piece in range(COLUMN_PIECES):
        for d in range(1, n_tp):
            moved[d, piece].wait_recv()
            swaps.append(swap(d, piece))
    send_over(blocks - 1)
    for copy in swaps:
        copy.wait_recv()
    for d in range(1, n_tp):
        for slot in range(4):
            load(wo_ref.at[d - 1, role_rows(slot)], slot, d)
    for copy in loads:
        copy.wait()
    strip = min(4 * SUB, out_cols)

    def project(block, carry):
        for copy in over_waits(block):
            copy.wait_recv()
        pairs = [(d, slot) for d in range(n_tp) for slot in range(4)]
        left = jnp.concatenate([full_ref[d, block, slot] for d, slot in pairs], axis=1)
        span = pl.ds(pl.multiple_of(block * lanes, lanes), lanes)

        def one(n, carry):
            right = jnp.concatenate(
                [
                    tok_ref[slot, span, pl.ds(pl.multiple_of(d * out_cols + n * strip, strip), strip)]
                    for d, slot in pairs
                ],
                axis=0,
            )
            value = jnp.dot(left, right, preferred_element_type=jnp.float32)
            where = pl.ds(pl.multiple_of(n * strip, strip), strip)

            @pl.when(block > 0)
            def _():
                total_ref[:, where] = total_ref[:, where] + value

            @pl.when(block == 0)
            def _():
                total_ref[:, where] = value

            return carry

        lax.fori_loop(0, out_cols // strip, one, 0)
        return carry

    lax.fori_loop(0, blocks, project, 0)
    mixed_ref[...] = total_ref[...].astype(mixed_ref.dtype)
    for copy in started:
        if all(copy is not other for other in inside):
            copy.wait_send()

    @pl.when(leads)
    def _():
        for copy in edges():
            copy.wait_send()

    def finish(block, carry):
        first(block).wait_send()
        for hop in hops:
            line(block, hop).wait_send()
            passing(block, hop).wait_send()
        for copy in shares(block) + roles(block):
            copy.wait_send()
        for n in range(4):
            for copy in overs(block, n):
                copy.wait_send()
        return carry

    lax.fori_loop(0, blocks, finish, 0)


def hyena(own, w3, w_out, taps, lags, leave, reach, fade, skip, by_mode, width):
    size, n_tp = lax.axis_size("seq"), lax.axis_size("tp")
    line, depth = size // 2, size // 4
    count = own.shape[0]
    chans = w3.shape[2] // 4
    lanes = min(BLOCK, chans)
    blocks = chans // lanes
    order = by_mode.shape[0]
    tall = HALO + count
    out_cols = w_out.shape[1] // n_tp
    anywhere = pl.BlockSpec(memory_space=pl.ANY)
    near = pl.BlockSpec(memory_space=pltpu.VMEM)
    counts = (
        [1 + 4 * n_tp, blocks] + [(blocks, line)] * 4 + [2, 2] + [2 * n_tp] * 4 + [0, 0]
        + [COLUMN_PIECES * n_tp] * 4 + [4, 2]
        + [(blocks, depth - 1)] * 2 + [(blocks, 3)] * 2 + [(blocks, 4 * n_tp)] * 2
    )
    return pl.pallas_call(
        functools.partial(hyena_kernel, width),
        out_shape=[
            jax.ShapeDtypeStruct((count, out_cols), jnp.bfloat16),
            jax.ShapeDtypeStruct((n_tp - 1, w_out.shape[0], out_cols), w_out.dtype),
        ],
        in_specs=[anywhere] * 3 + [near] * 7,
        out_specs=[near, anywhere],
        scratch_shapes=[
            pltpu.VMEM((4, tall, own.shape[1]), own.dtype),
            pltpu.VMEM((blocks, 3, own.shape[1], lanes), w3.dtype),
            pltpu.VMEM((4, tall, 3 * lanes), jnp.float32),
            pltpu.VMEM((4, tall, 3 * lanes), jnp.bfloat16),
            pltpu.VMEM((lanes // width * SUB, SUB), jnp.bfloat16),
            pltpu.VMEM((4, count, lanes), jnp.float32),
            pltpu.VMEM((4, count, lanes), jnp.float32),
            pltpu.VMEM((blocks, depth, 4, order, lanes), jnp.float32),
            pltpu.VMEM((blocks, 4, count, lanes), jnp.bfloat16),
            pltpu.VMEM((n_tp, blocks, 4, count, lanes), jnp.bfloat16),
            pltpu.VMEM((count, out_cols), jnp.float32),
        ]
        + [pltpu.SemaphoreType.DMA(n if isinstance(n, tuple) else (n,) if n else ()) for n in counts],
        compiler_params=pltpu.CompilerParams(
            collective_id=0, has_side_effects=True, vmem_limit_bytes=60 << 20
        ),
        name="hyena",
    )(own, w3, w_out, taps, lags, leave, reach, fade, skip, by_mode)[0]


def shards(tokens, w_in, short_taps, decay_rate, residue, skip_gain, w_out):
    count = tokens.shape[0]
    all_chans = w_in.shape[2]
    width = all_chans // decay_rate.shape[0]
    z, x, core, depth = place()
    role = 2 * lax.rem(z, 2) + core
    by_mode = jnp.repeat(decay_rate.T, width, axis=1)

    def own(array, axis):
        share = array.shape[axis] // 4
        return lax.dynamic_slice_in_dim(array, role * share, share, axis)

    decay_rate, residue = own(decay_rate, 0), own(residue, 0)
    groups, order = decay_rate.shape
    lanes = min(BLOCK, all_chans // 4)
    modes = lanes // width * order
    weight_mode = residue * jnp.sqrt(2.0 * decay_rate / order)
    offsets = jnp.arange(SUB, dtype=jnp.float32)
    back = (-jnp.arange(SUB) % SUB).astype(jnp.float32)
    lags = jnp.einsum(
        "gm,gmd->gd",
        weight_mode,
        jnp.exp(-decay_rate[:, :, None] * back[None, None, :]),
        precision=HIGHEST,
    )
    rate = decay_rate.reshape(groups * order)
    leave = jnp.exp(-rate[:, None] * (SUB - 1.0 - offsets[None, :]))
    fade = jnp.exp(-rate * SUB)[:, None]
    positions = jnp.arange(count, dtype=jnp.float32)
    rate = rate.reshape(-1, 1, modes)
    reach = weight_mode.reshape(-1, 1, modes) * jnp.exp(-rate * (positions[None, :, None] + 1.0))
    return hyena(
        tokens, w_in.transpose(1, 0, 2), w_out, short_taps, lags, leave, reach, fade,
        skip_gain[None], by_mode, width,
    )


def solution(mesh):
    in_specs = (
        P("seq", None),
        P("seq", None, "tp"),
        P(None, None, "tp"),
        P("tp", None),
        P("tp", None),
        P("tp"),
        P("tp", None),
    )
    out_specs = P("seq", "tp")
    return jax.shard_map(shards, mesh=mesh, in_specs=in_specs, out_specs=out_specs, check_vma=False)
```

```python
import functools

import jax
import jax.numpy as jnp
from jax import lax
from jax.experimental import pallas as pl
from jax.experimental.pallas import tpu as pltpu
from jax.sharding import PartitionSpec as P

SUB = 128
BLOCK = 128
COLUMN_PIECES = 8
HALO = 16
MESH = pl.DeviceIdType.MESH
HIGHEST = lax.Precision.HIGHEST


def shifted_by(block, axis, distance):
    devices = range(lax.axis_size(axis))
    route = [(i - distance, i) for i in devices if i - distance in devices]
    return lax.ppermute(block, axis, route)


def fanned(state, width, order):
    lanes = state.shape[1]
    tile = lanes // width
    full = jnp.concatenate([state] * tile, axis=0)
    row = lax.broadcasted_iota(jnp.int32, full.shape, 0) // order
    lane = lax.broadcasted_iota(jnp.int32, full.shape, 1) // width
    return jnp.where(row == lane, full, 0.0)


def split(value):
    high = value.astype(jnp.bfloat16)
    return high, (value - high.astype(jnp.float32)).astype(jnp.bfloat16)


def product_split(a, b):
    (ah, al), (bh, bl) = a, b
    dot = functools.partial(jnp.dot, preferred_element_type=jnp.float32)
    return dot(ah, bh) + (dot(ah, bl) + dot(al, bh))


def place():
    size, here = lax.axis_size("seq"), lax.axis_index("seq")
    return here // 4, lax.rem(here // 2, 2), lax.rem(here, 2), size // 4


def index_of(z, x, core):
    return z * 4 + x * 2 + core


def greet(peers):
    barrier = pltpu.get_barrier_semaphore()
    for peer in peers:
        pl.semaphore_signal(barrier, inc=1, device_id=peer, device_id_type=MESH)
    pl.semaphore_wait(barrier, len(peers))


def remote(source, target, send_sem, recv_sem, peer):
    return pltpu.make_async_remote_copy(
        src_ref=source,
        dst_ref=target,
        send_sem=send_sem,
        recv_sem=recv_sem,
        device_id=peer,
        device_id_type=MESH,
    )


def hyena_kernel(
    width,
    own_ref, w3_ref, out_ref, taps_ref, lags_ref, leave_ref, reach_ref, fade_ref, skip_ref, mode_ref,
    mixed_ref, wo_ref,
    tok_ref, w_ref, acc_ref, proj_ref, toep_ref, query_ref, base_ref, all_ref, mix_ref, full_ref, total_ref,
    local_sems, own_sems,
    line_send, line_recv, pass_send, pass_recv, pair_send, pair_recv,
    tp_send, tp_recv, core_send, core_recv, early_send, early_recv,
    cols_send, cols_recv, swap_send, swap_recv, halo_send, halo_recv,
    share_send, share_recv, role_send, role_recv, over_send, over_recv,
):
    z, x, core, depth = place()
    parity = lax.rem(z, 2)
    n_tp, part = lax.axis_size("tp"), lax.axis_index("tp")
    size = lax.axis_size("seq")
    mine = index_of(z, x, core)
    side = {"seq": index_of(z, 1 - x, core)}
    twin = {"seq": index_of(z, x, 1 - core)}
    blocks, _, _, lanes = w_ref.shape
    rows = w3_ref.shape[1]
    count = own_ref.shape[0]
    taps = taps_ref.shape[0]
    order = all_ref.shape[3]
    tile = lanes // width
    modes = tile * order

    def on_line(hop):
        there = z ^ hop[0]
        return there, (1 - core if hop[1] else core)

    hops = [(step, other) for step in range(depth) for other in range(2)][1:]
    tps = [{"tp": lax.rem(part + d, n_tp)} for d in range(1, n_tp)]
    greet([{"seq": lax.rem(mine + d, size)} for d in range(1, size)] + tps)

    cols = own_ref.shape[1] // (2 * n_tp)

    def band(which, piece):
        return pl.ds(pl.multiple_of((2 * which + piece) * cols, cols), cols)

    own_slot, mate_slot = 2 * parity + core, 2 * (1 - parity) + core
    body = pl.ds(HALO, count)
    edge = pl.ds(HALO // 2, HALO // 2)
    taken = pltpu.make_async_copy(own_ref, tok_ref.at[own_slot, body], local_sems.at[0])
    started = []

    def begin(*what):
        copy = remote(*what)
        copy.start()
        started.append(copy)
        return copy

    def wide(role, block):
        return w3_ref.at[:, :, pl.ds(pl.multiple_of((role * blocks + block) * lanes, lanes), lanes)]

    def landed(block, source):
        return w_ref.at[block, :, pl.ds(pl.multiple_of(source * rows, rows), rows), :]

    def own_piece(block):
        return pltpu.make_async_copy(wide(own_slot, block), landed(block, mine), own_sems.at[block])

    def first(block):
        return remote(
            wide(own_slot, block), landed(block, mine),
            pass_send.at[block, 0], pass_recv.at[block, 0], side,
        )

    def line(block, hop):
        there, which = on_line(hop)
        index = 2 * hop[0] + hop[1]
        return remote(
            wide(2 * lax.rem(there, 2) + which, block), landed(block, mine),
            line_send.at[block, index], line_recv.at[block, index], {"seq": index_of(there, x, which)},
        )

    def arriving(block, hop):
        there, which = on_line(hop)
        index = 2 * hop[0] + hop[1]
        where = landed(block, index_of(there, x, which))
        return remote(
            where, where, line_send.at[block, index], line_recv.at[block, index],
            {"seq": index_of(there, x, which)},
        )

    def passing(block, hop):
        there, which = on_line(hop)
        index = 2 * hop[0] + hop[1]
        where = landed(block, index_of(there, x, which))
        return remote(where, where, pass_send.at[block, index], pass_recv.at[block, index], side)

    def passed(block, hop):
        there, which = on_line(hop)
        index = 2 * hop[0] + hop[1]
        where = landed(block, index_of(there, 1 - x, which))
        return remote(where, where, pass_send.at[block, index], pass_recv.at[block, index], side)

    def to_pair(piece):
        where = tok_ref.at[own_slot, body, band(part, piece)]
        return begin(
            own_ref.at[:, band(part, piece)], where, pair_send.at[piece], pair_recv.at[piece],
            {"seq": index_of(z ^ 1, x, core)},
        )

    portion = wo_ref.shape[1] // (2 * COLUMN_PIECES)
    out_cols = wo_ref.shape[2]

    def portion_rows(piece):
        return pl.ds(pl.multiple_of((COLUMN_PIECES * core + piece) * portion, portion), portion)

    def out_span(which):
        return pl.ds(pl.multiple_of(which * out_cols, out_cols), out_cols)

    moved = {}

    def columns(pieces):
        for piece in pieces:
            for d in range(1, n_tp):
                slot = COLUMN_PIECES * (d - 1) + piece
                moved[d, piece] = begin(
                    out_ref.at[portion_rows(piece), out_span(lax.rem(part + d, n_tp))],
                    wo_ref.at[d - 1, portion_rows(piece)],
                    cols_send.at[slot], cols_recv.at[slot], tps[d - 1],
                )

    def swap(d, piece):
        slot = COLUMN_PIECES * (d - 1) + piece
        where = wo_ref.at[d - 1, portion_rows(piece)]
        return begin(where, where, swap_send.at[slot], swap_recv.at[slot], twin)

    after = jnp.where(x == 0, z, z + 1)
    leads = (core == 1) & ((x == 0) | (z < depth - 1))

    def edges():
        copies = []
        for n in range(4):
            slot = 2 * lax.rem(after, 2)
            copies.append(remote(
                own_ref.at[pl.ds(count - HALO // 2, HALO // 2)], tok_ref.at[slot, edge],
                halo_send.at[n], halo_recv.at[lax.rem(after, 2)],
                {"seq": index_of(after ^ (n // 2), 1 - x, n % 2)},
            ))
        return copies

    inner = (lax.rem(z, 4) == 1) | (lax.rem(z, 4) == 2)

    def step_of(turn):
        rolled = lax.rem(turn + depth - 3, depth - 1) + 1
        return jnp.where(inner & (turn > 0), rolled, turn)

    def forward(block, step):
        for other in range(2):
            arriving(block, (step, other)).wait_recv()
            passing(block, (step, other)).start()

    def forward_far(block, carry):
        forward(block, depth - 1)
        return carry

    def forward_slot(block, turn):
        outer = 2 - turn if turn < 2 else turn + 1

        @pl.when(jnp.logical_not(inner) | (turn < depth - 2))
        def _():
            forward(block, jnp.where(inner, turn + 1, outer))

    def near(block, carry):
        arriving(block, (0, 1)).wait_recv()
        passing(block, (0, 1)).start()
        return carry

    def begin_own(block, carry):
        own_piece(block).start()
        first(block).start()
        line(block, (0, 1)).start()
        return carry

    def issue_step(block, step):
        for other in range(2):
            line(block, (step, other)).start()

    def issue(block, begin_step=1):
        for step in range(begin_step, depth - 1):
            issue_step(block, step)

        @pl.when(jnp.logical_not(inner))
        def _():
            issue_step(block, depth - 1)

    def issue_far(block, carry):
        issue_step(block, depth - 1)
        return carry

    paired = [to_pair(0), to_pair(1)]
    columns(range(2))
    lax.fori_loop(0, blocks, begin_own, 0)

    @pl.when(leads)
    def _():
        for copy in edges():
            copy.start()

    @pl.when(inner)
    def _():
        lax.fori_loop(0, blocks, issue_far, 0)
        issue_step(0, 1)

    @pl.when(jnp.logical_not(inner))
    def _():
        issue(0)

    early = begin(own_ref, tok_ref.at[own_slot, body], early_send, early_recv, twin)
    taken.start()
    twins, across = [], {}

    def to_twin(which, piece, d):
        where = tok_ref.at[mate_slot, body, band(which, piece)]
        slot = 2 * d + piece
        twins.append(begin(where, where, core_send.at[slot], core_recv.at[slot], twin))

    def pair_on(piece):
        paired[piece].wait_recv()
        where = tok_ref.at[mate_slot, body, band(part, piece)]
        for d in range(1, n_tp):
            slot = 2 * (d - 1) + piece
            across[d, piece] = begin(
                where, where, tp_send.at[slot], tp_recv.at[slot], tps[d - 1]
            )
        to_twin(part, piece, 0)

    lax.fori_loop(0, blocks, near, 0)
    half = blocks // 2

    @pl.when(inner)
    def _():
        lax.fori_loop(0, half, forward_far, 0)

    pair_on(0)
    columns(range(2, 4))

    @pl.when(inner)
    def _():
        lax.fori_loop(half, blocks, forward_far, 0)

    pair_on(1)
    columns(range(4, COLUMN_PIECES))

    @pl.when(inner)
    def _():
        for n in range(2, depth - 1):
            issue_step(0, n)

    if blocks > 1:
        issue(1)

    def tokens_on(piece):
        for d in range(1, n_tp):
            across[d, piece].wait_recv()
            to_twin(lax.rem(part - d + n_tp, n_tp), piece, d)

    tokens_on(0)
    forward_slot(0, 0)
    forward_slot(0, 1)
    tokens_on(1)
    taken.wait()
    for copy in [early] + twins:
        copy.wait_recv()
    for p in range(2):
        starts = (z - parity + p == 0) & (x == 0)

        @pl.when(starts)
        def _():
            tok_ref[2 * p, HALO // 2 : HALO] = jnp.zeros(
                (HALO // 2, tok_ref.shape[2]), tok_ref.dtype
            )

        @pl.when(jnp.logical_not(starts))
        def _():
            where = tok_ref.at[2 * p, edge]
            remote(where, where, halo_send.at[0], halo_recv.at[p], side).wait_recv()

        tok_ref[2 * p + 1, HALO // 2 : HALO] = tok_ref[2 * p, HALO // 2 + count : HALO + count]

    depth_rows = 4 * rows

    def compute(block, turn):
        step = step_of(turn)

        @pl.when(step == 0)
        def _():
            own_piece(block).wait()

        for other in range(2):
            passed(block, (step, other)).wait_recv()
        span = pl.ds(pl.multiple_of((z ^ step) * depth_rows, depth_rows), depth_rows)

        def one(slot, carry):
            right = jnp.concatenate([w_ref[block, p, span, :] for p in range(3)], axis=1)
            value = jnp.dot(tok_ref[slot, :, span], right, preferred_element_type=jnp.float32)

            @pl.when(step == 0)
            def _():
                acc_ref[slot] = value

            @pl.when(step != 0)
            def _():
                acc_ref[slot] = acc_ref[slot] + value

            return carry

        lax.fori_loop(0, 4, one, 0)

        @pl.when(turn == depth - 1)
        def _():
            def put(slot, carry):
                proj_ref[slot] = acc_ref[slot].astype(proj_ref.dtype)
                return carry

            lax.fori_loop(0, 4, put, 0)

    team = (z // 2) * 2 + x
    lane = lax.broadcasted_iota(jnp.int32, (SUB, 2 * lanes), 1)
    lane = lax.rem(lane, lanes) // width
    diagonal = (
        lax.broadcasted_iota(jnp.int32, (modes, lanes), 0) // order
        == lax.broadcasted_iota(jnp.int32, (modes, lanes), 1) // width
    )

    def chan(block):
        return pl.ds(pl.multiple_of((own_slot * blocks + block) * lanes, lanes), lanes)

    def prepare(block):
        below = lax.broadcasted_iota(jnp.int32, (SUB, SUB), 0) >= lax.broadcasted_iota(
            jnp.int32, (SUB, SUB), 1
        )
        lags = lags_ref[pl.ds(pl.multiple_of(block * tile, tile), tile)]
        for g in range(tile):
            turned = pltpu.roll(
                jnp.broadcast_to(lags[g : g + 1], (SUB, SUB)), 0, 1, stride=1, stride_axis=0
            )
            toep_ref[g * SUB : (g + 1) * SUB] = jnp.where(below, turned, 0.0).astype(jnp.bfloat16)

    def convolve(block, begin_slot, end_slot):
        span = pl.ds(pl.multiple_of(block * modes, modes), modes)
        leave = split(leave_ref[span])
        reach = split(reach_ref[block, :SUB])
        fade = fade_ref[span]
        skip = skip_ref[:, chan(block)]
        skip = jnp.concatenate([skip, skip], axis=1)
        kernel_taps = [[taps_ref[tap, w : w + 1, chan(block)] for w in range(3)] for tap in range(taps)]

        def segment(slot, carry):
            def filtered(which):
                value = proj_ref[slot, :, which * lanes : (which + 1) * lanes].astype(jnp.float32)
                out = None
                for tap in range(taps):
                    term = kernel_taps[tap][which] * value[HALO - tap : HALO - tap + count]
                    out = term if out is None else out + term
                return out

            query_ref[slot] = filtered(0)
            gated = filtered(1) * filtered(2)
            state = jnp.zeros((modes, lanes), jnp.float32)
            for two in range(count // SUB // 2):
                low, high = 2 * two * SUB, (2 * two + 1) * SUB
                piece = jnp.concatenate([gated[low:high], gated[high : high + SUB]], axis=1)
                spread = jnp.dot(
                    toep_ref[...], piece.astype(jnp.bfloat16), preferred_element_type=jnp.float32
                )
                picked = spread[:SUB]
                for g in range(1, tile):
                    picked = jnp.where(lane == g, spread[g * SUB : (g + 1) * SUB], picked)
                local = skip * piece + picked
                fresh = product_split(leave, split(piece))
                for turn, start in ((0, low), (1, high)):
                    value = local[:, turn * lanes : (turn + 1) * lanes]
                    if start:
                        value = value + product_split(reach, split(state))
                    base_ref[slot, start : start + SUB] = value
                    state = fade * state + jnp.where(
                        diagonal, fresh[:, turn * lanes : (turn + 1) * lanes], 0.0
                    )
            compact = state[:order]
            for g in range(1, tile):
                compact = compact + state[g * order : (g + 1) * order]
            all_ref[block, team, slot] = compact
            return carry

        lax.fori_loop(begin_slot, end_slot, segment, 0)

    def teammate(d):
        there = lax.rem(team + d, depth)
        return there, {
            "seq": index_of(2 * (there // 2) + parity, lax.rem(there, 2), core)
        }

    def shares(block):
        return [
            remote(
                all_ref.at[block, team], all_ref.at[block, team],
                share_send.at[block, d - 1], share_recv.at[block, d - 1], teammate(d)[1],
            )
            for d in range(1, depth)
        ]

    def share_waits(block):
        return [
            remote(
                all_ref.at[block, lax.rem(team - d + depth, depth)],
                all_ref.at[block, lax.rem(team - d + depth, depth)],
                share_send.at[block, d - 1], share_recv.at[block, d - 1], teammate(d)[1],
            )
            for d in range(1, depth)
        ]

    def colleague(d):
        there, which = z ^ (d // 2), (1 - core if d % 2 else core)
        return 2 * lax.rem(there, 2) + which, {"seq": index_of(there, x, which)}

    def combine(block):
        for copy in share_waits(block):
            copy.wait_recv()
        rates = mode_ref[:, chan(block)]
        reach = split(reach_ref[block])

        def segment(slot, carry):
            here = index_of(z - parity + slot // 2, x, lax.rem(slot, 2))

            def member(n, entering):
                for other in range(4):
                    ahead = here - 1 - index_of(
                        2 * (n // 2) + other // 2, lax.rem(n, 2), other % 2
                    )
                    far = (count * jnp.maximum(ahead, 0)).astype(jnp.float32)
                    weight = jnp.where(ahead >= 0, jnp.exp(-rates * far), 0.0)
                    entering = entering + weight * all_ref[block, n, other]
                return entering

            entering = lax.fori_loop(0, depth, member, jnp.zeros((order, lanes), jnp.float32))
            carried = product_split(reach, split(fanned(entering, width, order)))
            mix_ref[block, slot] = (query_ref[slot] * (base_ref[slot] + carried)).astype(mix_ref.dtype)
            return carry

        lax.fori_loop(0, 4, segment, 0)
        full_ref[0, block, own_slot] = mix_ref[block, own_slot]

    def roles(block):
        return [
            remote(
                mix_ref.at[block, colleague(d)[0]], full_ref.at[0, block, own_slot],
                role_send.at[block, d - 1], role_recv.at[block, d - 1], colleague(d)[1],
            )
            for d in (2, 3, 1)
        ]

    def role_waits(block):
        return [
            remote(
                full_ref.at[0, block, colleague(d)[0]], full_ref.at[0, block, colleague(d)[0]],
                role_send.at[block, d - 1], role_recv.at[block, d - 1], colleague(d)[1],
            )
            for d in range(1, 4)
        ]

    def overs(block, n):
        which = colleague(n)[0]
        return [
            remote(
                full_ref.at[0, block, which], full_ref.at[d, block, which],
                over_send.at[block, 4 * (d - 1) + n], over_recv.at[block, 4 * (d - 1) + n], tps[d - 1],
            )
            for d in range(1, n_tp)
        ]

    def over_waits(block):
        return [
            remote(
                full_ref.at[d, block, colleague(n)[0]], full_ref.at[d, block, colleague(n)[0]],
                over_send.at[block, 4 * (d - 1) + n], over_recv.at[block, 4 * (d - 1) + n], tps[d - 1],
            )
            for n in range(4)
            for d in range(1, n_tp)
        ]

    def send_states(block):
        for copy in shares(block):
            copy.start()

    def send_mix(block):
        for copy in roles(block) + overs(block, 0):
            copy.start()

    def send_over(block):
        for n, copy in enumerate(role_waits(block)):
            copy.wait_recv()
            for across_copy in overs(block, n + 1):
                across_copy.start()

    def stage(block, carry):
        @pl.when(block > 0)
        def _():
            forward_slot(block, 0)
            compute(block - 1, depth - 1)
            prepare(block - 1)
            convolve(block - 1, 0, 4)
            send_states(block - 1)

            @pl.when(block + 1 < blocks)
            def _():
                issue(block + 1)

            forward_slot(block, 1)

        compute(block, 0)
        for turn in range(2, depth - 1):
            forward_slot(block, turn)
        compute(block, 1)

        @pl.when(block > 0)
        def _():
            combine(block - 1)
            send_mix(block - 1)

        for turn in range(2, depth - 1):
            compute(block, turn)

        @pl.when(block > 1)
        def _():
            send_over(block - 2)

        return carry

    lax.fori_loop(0, blocks, stage, 0)
    swaps = []
    for piece in range(COLUMN_PIECES):
        for d in range(1, n_tp):
            moved[d, piece].wait_recv()
            swaps.append(swap(d, piece))
    compute(blocks - 1, depth - 1)
    if blocks > 1:
        send_over(blocks - 2)
    loads = []

    def load(source, slot, d):
        chans = blocks * lanes
        copy = pltpu.make_async_copy(
            source, tok_ref.at[slot, pl.ds(0, chans), pl.ds(d * out_cols, out_cols)],
            local_sems.at[1 + 4 * d + slot],
        )
        copy.start()
        loads.append(copy)

    def role_rows(slot):
        return pl.ds(slot * blocks * lanes, blocks * lanes)

    inside = twins + list(across.values())
    for copy in inside:
        copy.wait_send()
    for slot in range(4):
        load(out_ref.at[role_rows(slot), out_span(part)], slot, 0)
    prepare(blocks - 1)
    convolve(blocks - 1, 0, 4)
    send_states(blocks - 1)
    for copy in swaps:
        copy.wait_recv()
    for d in range(1, n_tp):
        for slot in range(4):
            load(wo_ref.at[d - 1, role_rows(slot)], slot, d)
    for copy in loads:
        copy.wait()
    strip = min(4 * SUB, out_cols)

    def project(block, carry):
        for copy in over_waits(block):
            copy.wait_recv()
        pairs = [(d, slot) for d in range(n_tp) for slot in range(4)]
        left = jnp.concatenate([full_ref[d, block, slot] for d, slot in pairs], axis=1)
        span = pl.ds(pl.multiple_of(block * lanes, lanes), lanes)

        def one(n, carry):
            right = jnp.concatenate(
                [
                    tok_ref[slot, span, pl.ds(pl.multiple_of(d * out_cols + n * strip, strip), strip)]
                    for d, slot in pairs
                ],
                axis=0,
            )
            value = jnp.dot(left, right, preferred_element_type=jnp.float32)
            where = pl.ds(pl.multiple_of(n * strip, strip), strip)

            @pl.when(block > 0)
            def _():
                total_ref[:, where] = total_ref[:, where] + value

            @pl.when(block == 0)
            def _():
                total_ref[:, where] = value

            return carry

        lax.fori_loop(0, out_cols // strip, one, 0)
        return carry

    lax.fori_loop(0, half, project, 0)
    combine(blocks - 1)
    send_mix(blocks - 1)
    send_over(blocks - 1)
    lax.fori_loop(half, blocks, project, 0)
    mixed_ref[...] = total_ref[...].astype(mixed_ref.dtype)
    for copy in started:
        if all(copy is not other for other in inside):
            copy.wait_send()

    @pl.when(leads)
    def _():
        for copy in edges():
            copy.wait_send()

    def finish(block, carry):
        first(block).wait_send()
        for hop in hops:
            line(block, hop).wait_send()
            passing(block, hop).wait_send()
        for copy in shares(block) + roles(block):
            copy.wait_send()
        for n in range(4):
            for copy in overs(block, n):
                copy.wait_send()
        return carry

    lax.fori_loop(0, blocks, finish, 0)


def hyena(own, w3, w_out, taps, lags, leave, reach, fade, skip, by_mode, width):
    size, n_tp = lax.axis_size("seq"), lax.axis_size("tp")
    line, depth = size // 2, size // 4
    count = own.shape[0]
    chans = w3.shape[2] // 4
    lanes = min(BLOCK, chans)
    blocks = chans // lanes
    order = by_mode.shape[0]
    tall = HALO + count
    out_cols = w_out.shape[1] // n_tp
    anywhere = pl.BlockSpec(memory_space=pl.ANY)
    near = pl.BlockSpec(memory_space=pltpu.VMEM)
    counts = (
        [1 + 4 * n_tp, blocks] + [(blocks, line)] * 4 + [2, 2] + [2 * n_tp] * 4 + [0, 0]
        + [COLUMN_PIECES * n_tp] * 4 + [4, 2]
        + [(blocks, depth - 1)] * 2 + [(blocks, 3)] * 2 + [(blocks, 4 * n_tp)] * 2
    )
    return pl.pallas_call(
        functools.partial(hyena_kernel, width),
        out_shape=[
            jax.ShapeDtypeStruct((count, out_cols), jnp.bfloat16),
            jax.ShapeDtypeStruct((n_tp - 1, w_out.shape[0], out_cols), w_out.dtype),
        ],
        in_specs=[anywhere] * 3 + [near] * 7,
        out_specs=[near, anywhere],
        scratch_shapes=[
            pltpu.VMEM((4, tall, own.shape[1]), own.dtype),
            pltpu.VMEM((blocks, 3, own.shape[1], lanes), w3.dtype),
            pltpu.VMEM((4, tall, 3 * lanes), jnp.float32),
            pltpu.VMEM((4, tall, 3 * lanes), jnp.bfloat16),
            pltpu.VMEM((lanes // width * SUB, SUB), jnp.bfloat16),
            pltpu.VMEM((4, count, lanes), jnp.float32),
            pltpu.VMEM((4, count, lanes), jnp.float32),
            pltpu.VMEM((blocks, depth, 4, order, lanes), jnp.float32),
            pltpu.VMEM((blocks, 4, count, lanes), jnp.bfloat16),
            pltpu.VMEM((n_tp, blocks, 4, count, lanes), jnp.bfloat16),
            pltpu.VMEM((count, out_cols), jnp.float32),
        ]
        + [pltpu.SemaphoreType.DMA(n if isinstance(n, tuple) else (n,) if n else ()) for n in counts],
        compiler_params=pltpu.CompilerParams(
            collective_id=0, has_side_effects=True, vmem_limit_bytes=60 << 20
        ),
        name="hyena",
    )(own, w3, w_out, taps, lags, leave, reach, fade, skip, by_mode)[0]


def shards(tokens, w_in, short_taps, decay_rate, residue, skip_gain, w_out):
    count = tokens.shape[0]
    all_chans = w_in.shape[2]
    width = all_chans // decay_rate.shape[0]
    z, x, core, depth = place()
    role = 2 * lax.rem(z, 2) + core
    by_mode = jnp.repeat(decay_rate.T, width, axis=1)

    def own(array, axis):
        share = array.shape[axis] // 4
        return lax.dynamic_slice_in_dim(array, role * share, share, axis)

    decay_rate, residue = own(decay_rate, 0), own(residue, 0)
    groups, order = decay_rate.shape
    lanes = min(BLOCK, all_chans // 4)
    modes = lanes // width * order
    weight_mode = residue * jnp.sqrt(2.0 * decay_rate / order)
    offsets = jnp.arange(SUB, dtype=jnp.float32)
    back = (-jnp.arange(SUB) % SUB).astype(jnp.float32)
    lags = jnp.einsum(
        "gm,gmd->gd",
        weight_mode,
        jnp.exp(-decay_rate[:, :, None] * back[None, None, :]),
        precision=HIGHEST,
    )
    rate = decay_rate.reshape(groups * order)
    leave = jnp.exp(-rate[:, None] * (SUB - 1.0 - offsets[None, :]))
    fade = jnp.exp(-rate * SUB)[:, None]
    positions = jnp.arange(count, dtype=jnp.float32)
    rate = rate.reshape(-1, 1, modes)
    reach = weight_mode.reshape(-1, 1, modes) * jnp.exp(-rate * (positions[None, :, None] + 1.0))
    return hyena(
        tokens, w_in.transpose(1, 0, 2), w_out, short_taps, lags, leave, reach, fade,
        skip_gain[None], by_mode, width,
    )


def solution(mesh):
    in_specs = (
        P("seq", None),
        P("seq", None, "tp"),
        P(None, None, "tp"),
        P("tp", None),
        P("tp", None),
        P("tp"),
        P("tp", None),
    )
    out_specs = P("seq", "tp")
    return jax.shard_map(shards, mesh=mesh, in_specs=in_specs, out_specs=out_specs, check_vma=False)
```

```python
import functools

import jax
import jax.numpy as jnp
from jax import lax
from jax.experimental import pallas as pl
from jax.experimental.pallas import tpu as pltpu
from jax.sharding import PartitionSpec as P

SUB = 128
BLOCK = 128
COLUMN_PIECES = 8
HALO = 16
MESH = pl.DeviceIdType.MESH


def fanned(state, width, order):
    lanes = state.shape[1]
    tile = lanes // width
    full = jnp.concatenate([state] * tile, axis=0)
    row = lax.broadcasted_iota(jnp.int32, full.shape, 0) // order
    lane = lax.broadcasted_iota(jnp.int32, full.shape, 1) // width
    return jnp.where(row == lane, full, 0.0)


def split(value):
    high = value.astype(jnp.bfloat16)
    return high, (value - high.astype(jnp.float32)).astype(jnp.bfloat16)


def product_split(a, b):
    (ah, al), (bh, bl) = a, b
    dot = functools.partial(jnp.dot, preferred_element_type=jnp.float32)
    return dot(ah, bh) + (dot(ah, bl) + dot(al, bh))


def place():
    size, here = lax.axis_size("seq"), lax.axis_index("seq")
    return here // 4, lax.rem(here // 2, 2), lax.rem(here, 2), size // 4


def index_of(z, x, core):
    return z * 4 + x * 2 + core


def greet(peers):
    barrier = pltpu.get_barrier_semaphore()
    for peer in peers:
        pl.semaphore_signal(barrier, inc=1, device_id=peer, device_id_type=MESH)
    pl.semaphore_wait(barrier, len(peers))


def remote(source, target, send_sem, recv_sem, peer):
    return pltpu.make_async_remote_copy(
        src_ref=source,
        dst_ref=target,
        send_sem=send_sem,
        recv_sem=recv_sem,
        device_id=peer,
        device_id_type=MESH,
    )


def coefficients(
    width, role, decay_ref, residue_ref, lags_ref, leave_ref, reach_ref, fade_ref, mode_ref
):
    order = decay_ref.shape[0]
    groups = decay_ref.shape[1] // 4
    blocks, _, lanes = mode_ref.shape
    count, modes = reach_ref.shape[1:]

    def own(ref):
        whole = ref[...]
        part = whole[:, :groups]
        for n in range(1, 4):
            part = jnp.where(role == n, whole[:, n * groups : (n + 1) * groups], part)
        return part

    rate = own(decay_ref)
    gain = own(residue_ref) * jnp.sqrt(2.0 * rate / order)
    place_in = lax.broadcasted_iota(jnp.int32, (order, SUB), 1)
    back = jnp.where(place_in == 0, 0, SUB - place_in).astype(jnp.float32)
    left = (SUB - 1 - place_in).astype(jnp.float32)
    rows = lax.broadcasted_iota(jnp.int32, (order, modes), 0)
    lane = lax.broadcasted_iota(jnp.int32, (order, modes), 1)
    wide = lax.broadcasted_iota(jnp.int32, (order, lanes), 1) // width
    later = lax.broadcasted_iota(jnp.int32, (count, modes), 0).astype(jnp.float32) + 1.0
    per = lanes // width
    for block in range(blocks):
        by_rate = jnp.zeros((order, modes), jnp.float32)
        by_gain = jnp.zeros((order, modes), jnp.float32)
        by_lane = jnp.zeros((order, lanes), jnp.float32)
        for n in range(per):
            g = block * per + n
            column = rate[:, g : g + 1]
            strength = gain[:, g : g + 1]
            span = slice(g * order, (g + 1) * order)
            lags_ref[g : g + 1] = jnp.sum(strength * jnp.exp(-column * back), axis=0, keepdims=True)
            leave_ref[span] = jnp.exp(-column * left)
            fade_ref[span] = jnp.exp(-jnp.broadcast_to(column, (order, lanes)) * SUB)
            by_rate = jnp.where(lane // order == n, column, by_rate)
            by_gain = jnp.where(lane // order == n, strength, by_gain)
            by_lane = jnp.where(wide == n, column, by_lane)
        mode_ref[block] = by_lane
        pick = rows == lax.rem(lane, order)
        flat = jnp.sum(jnp.where(pick, by_rate, 0.0), axis=0, keepdims=True)
        weight = jnp.sum(jnp.where(pick, by_gain, 0.0), axis=0, keepdims=True)
        reach_ref[block] = weight * jnp.exp(-flat * later)


def hyena_kernel(
    width,
    own_ref, w3_ref, out_ref, taps_ref, decay_ref, residue_ref, skip_ref,
    mixed_ref, wo_ref,
    lags_ref, leave_ref, reach_ref, fade_ref, mode_ref, tok_ref, w_ref, acc_ref, proj_ref, toep_ref, query_ref, base_ref, all_ref, mix_ref, full_ref, total_ref,
    local_sems, own_sems,
    line_send, line_recv, pass_send, pass_recv, pair_send, pair_recv,
    tp_send, tp_recv, core_send, core_recv, early_send, early_recv,
    cols_send, cols_recv, swap_send, swap_recv, halo_send, halo_recv,
    share_send, share_recv, role_send, role_recv, over_send, over_recv,
):
    z, x, core, depth = place()
    parity = lax.rem(z, 2)
    n_tp, part = lax.axis_size("tp"), lax.axis_index("tp")
    size = lax.axis_size("seq")
    mine = index_of(z, x, core)
    side = {"seq": index_of(z, 1 - x, core)}
    twin = {"seq": index_of(z, x, 1 - core)}
    blocks, _, _, lanes = w_ref.shape
    rows = w3_ref.shape[1]
    count = own_ref.shape[0]
    taps = taps_ref.shape[0]
    order = all_ref.shape[3]
    tile = lanes // width
    modes = tile * order

    def on_line(hop):
        there = z ^ hop[0]
        return there, (1 - core if hop[1] else core)

    hops = [(step, other) for step in range(depth) for other in range(2)][1:]
    tps = [{"tp": lax.rem(part + d, n_tp)} for d in range(1, n_tp)]
    greet([{"seq": lax.rem(mine + d, size)} for d in range(1, size)] + tps)

    cols = own_ref.shape[1] // (2 * n_tp)

    def band(which, piece):
        return pl.ds(pl.multiple_of((2 * which + piece) * cols, cols), cols)

    own_slot, mate_slot = 2 * parity + core, 2 * (1 - parity) + core
    body = pl.ds(HALO, count)
    edge = pl.ds(HALO // 2, HALO // 2)
    taken = pltpu.make_async_copy(own_ref, tok_ref.at[own_slot, body], local_sems.at[0])
    started = []

    def begin(*what):
        copy = remote(*what)
        copy.start()
        started.append(copy)
        return copy

    def wide(role, block):
        return w3_ref.at[:, :, pl.ds(pl.multiple_of((role * blocks + block) * lanes, lanes), lanes)]

    def landed(block, source):
        return w_ref.at[block, :, pl.ds(pl.multiple_of(source * rows, rows), rows), :]

    def own_piece(block):
        return pltpu.make_async_copy(wide(own_slot, block), landed(block, mine), own_sems.at[block])

    def first(block):
        return remote(
            wide(own_slot, block), landed(block, mine),
            pass_send.at[block, 0], pass_recv.at[block, 0], side,
        )

    def line(block, hop):
        there, which = on_line(hop)
        index = 2 * hop[0] + hop[1]
        return remote(
            wide(2 * lax.rem(there, 2) + which, block), landed(block, mine),
            line_send.at[block, index], line_recv.at[block, index], {"seq": index_of(there, x, which)},
        )

    def arriving(block, hop):
        there, which = on_line(hop)
        index = 2 * hop[0] + hop[1]
        where = landed(block, index_of(there, x, which))
        return remote(
            where, where, line_send.at[block, index], line_recv.at[block, index],
            {"seq": index_of(there, x, which)},
        )

    def passing(block, hop):
        there, which = on_line(hop)
        index = 2 * hop[0] + hop[1]
        where = landed(block, index_of(there, x, which))
        return remote(where, where, pass_send.at[block, index], pass_recv.at[block, index], side)

    def passed(block, hop):
        there, which = on_line(hop)
        index = 2 * hop[0] + hop[1]
        where = landed(block, index_of(there, 1 - x, which))
        return remote(where, where, pass_send.at[block, index], pass_recv.at[block, index], side)

    def to_pair(piece):
        where = tok_ref.at[own_slot, body, band(part, piece)]
        return begin(
            own_ref.at[:, band(part, piece)], where, pair_send.at[piece], pair_recv.at[piece],
            {"seq": index_of(z ^ 1, x, core)},
        )

    portion = wo_ref.shape[1] // (2 * COLUMN_PIECES)
    out_cols = wo_ref.shape[2]

    def portion_rows(piece):
        return pl.ds(pl.multiple_of((COLUMN_PIECES * core + piece) * portion, portion), portion)

    def out_span(which):
        return pl.ds(pl.multiple_of(which * out_cols, out_cols), out_cols)

    moved = {}

    def columns(pieces):
        for piece in pieces:
            for d in range(1, n_tp):
                slot = COLUMN_PIECES * (d - 1) + piece
                moved[d, piece] = begin(
                    out_ref.at[portion_rows(piece), out_span(lax.rem(part + d, n_tp))],
                    wo_ref.at[d - 1, portion_rows(piece)],
                    cols_send.at[slot], cols_recv.at[slot], tps[d - 1],
                )

    def swap(d, piece):
        slot = COLUMN_PIECES * (d - 1) + piece
        where = wo_ref.at[d - 1, portion_rows(piece)]
        return begin(where, where, swap_send.at[slot], swap_recv.at[slot], twin)

    after = jnp.where(x == 0, z, z + 1)
    leads = (core == 1) & ((x == 0) | (z < depth - 1))

    def edges():
        copies = []
        for n in range(4):
            slot = 2 * lax.rem(after, 2)
            copies.append(remote(
                own_ref.at[pl.ds(count - HALO // 2, HALO // 2)], tok_ref.at[slot, edge],
                halo_send.at[n], halo_recv.at[lax.rem(after, 2)],
                {"seq": index_of(after ^ (n // 2), 1 - x, n % 2)},
            ))
        return copies

    inner = (lax.rem(z, 4) == 1) | (lax.rem(z, 4) == 2)

    def step_of(turn):
        if turn == 0:
            return 0
        return jnp.where(
            inner, (turn + depth - 3) % (depth - 1) + 1, 3 - turn if turn < 3 else turn
        )

    def forward(block, step):
        for other in range(2):
            arriving(block, (step, other)).wait_recv()
            passing(block, (step, other)).start()

    def forward_far(block, carry):
        forward(block, depth - 1)
        return carry

    def forward_slot(block, turn):
        outer = 2 - turn if turn < 2 else turn + 1

        @pl.when(jnp.logical_not(inner) | (turn < depth - 2))
        def _():
            forward(block, jnp.where(inner, turn + 1, outer))

    def near(block, carry):
        arriving(block, (0, 1)).wait_recv()
        passing(block, (0, 1)).start()
        return carry

    def begin_own(block, carry):
        own_piece(block).start()
        first(block).start()
        line(block, (0, 1)).start()
        return carry

    def issue_step(block, step):
        for other in range(2):
            line(block, (step, other)).start()

    def issue(block, begin_step=1):
        for step in range(begin_step, depth - 1):
            issue_step(block, step)

        @pl.when(jnp.logical_not(inner))
        def _():
            issue_step(block, depth - 1)

    def issue_far(block, carry):
        issue_step(block, depth - 1)
        return carry

    paired = [to_pair(0), to_pair(1)]
    columns(range(2))
    lax.fori_loop(0, blocks, begin_own, 0)

    @pl.when(leads)
    def _():
        for copy in edges():
            copy.start()

    @pl.when(inner)
    def _():
        lax.fori_loop(0, blocks, issue_far, 0)
        issue_step(0, 1)

    @pl.when(jnp.logical_not(inner))
    def _():
        issue(0)

    early = begin(own_ref, tok_ref.at[own_slot, body], early_send, early_recv, twin)
    taken.start()
    twins, across = [], {}

    def to_twin(which, piece, d):
        where = tok_ref.at[mate_slot, body, band(which, piece)]
        slot = 2 * d + piece
        twins.append(begin(where, where, core_send.at[slot], core_recv.at[slot], twin))

    def pair_on(piece):
        paired[piece].wait_recv()
        where = tok_ref.at[mate_slot, body, band(part, piece)]
        for d in range(1, n_tp):
            slot = 2 * (d - 1) + piece
            across[d, piece] = begin(
                where, where, tp_send.at[slot], tp_recv.at[slot], tps[d - 1]
            )
        to_twin(part, piece, 0)

    lax.fori_loop(0, blocks, near, 0)
    coefficients(
        width, own_slot, decay_ref, residue_ref, lags_ref, leave_ref, reach_ref, fade_ref, mode_ref
    )
    half = blocks // 2

    @pl.when(inner)
    def _():
        lax.fori_loop(0, half, forward_far, 0)

    pair_on(0)

    @pl.when(inner)
    def _():
        lax.fori_loop(half, blocks, forward_far, 0)

    pair_on(1)
    columns(range(2, COLUMN_PIECES))

    @pl.when(inner)
    def _():
        for n in range(2, depth - 1):
            issue_step(0, n)

    if blocks > 1:
        issue(1)

    def tokens_on(piece):
        for d in range(1, n_tp):
            across[d, piece].wait_recv()
            to_twin(lax.rem(part - d + n_tp, n_tp), piece, d)

    tokens_on(0)
    forward_slot(0, 0)
    forward_slot(0, 1)
    tokens_on(1)
    taken.wait()
    for copy in [early] + twins:
        copy.wait_recv()
    for p in range(2):
        starts = (z - parity + p == 0) & (x == 0)

        @pl.when(starts)
        def _():
            tok_ref[2 * p, HALO // 2 : HALO] = jnp.zeros(
                (HALO // 2, tok_ref.shape[2]), tok_ref.dtype
            )

        @pl.when(jnp.logical_not(starts))
        def _():
            where = tok_ref.at[2 * p, edge]
            remote(where, where, halo_send.at[0], halo_recv.at[p], side).wait_recv()

        tok_ref[2 * p + 1, HALO // 2 : HALO] = tok_ref[2 * p, HALO // 2 + count : HALO + count]

    depth_rows = 4 * rows

    def compute(block, turn):
        step = step_of(turn)

        if turn == 0:
            own_piece(block).wait()

        for other in range(2):
            passed(block, (step, other)).wait_recv()
        span = pl.ds(pl.multiple_of((z ^ step) * depth_rows, depth_rows), depth_rows)

        def one(slot, carry):
            right = jnp.concatenate([w_ref[block, p, span, :] for p in range(3)], axis=1)
            value = jnp.dot(tok_ref[slot, :, span], right, preferred_element_type=jnp.float32)

            acc_ref[slot] = value if turn == 0 else acc_ref[slot] + value
            return carry

        lax.fori_loop(0, 4, one, 0)

        if turn == depth - 1:

            def put(slot, carry):
                proj_ref[slot] = acc_ref[slot].astype(proj_ref.dtype)
                return carry

            lax.fori_loop(0, 4, put, 0)

    team = (z // 2) * 2 + x
    lane = lax.broadcasted_iota(jnp.int32, (SUB, 2 * lanes), 1)
    lane = lax.rem(lane, lanes) // width
    diagonal = (
        lax.broadcasted_iota(jnp.int32, (modes, lanes), 0) // order
        == lax.broadcasted_iota(jnp.int32, (modes, lanes), 1) // width
    )

    def chan(block):
        return pl.ds(pl.multiple_of((own_slot * blocks + block) * lanes, lanes), lanes)

    def prepare(block):
        below = lax.broadcasted_iota(jnp.int32, (SUB, SUB), 0) >= lax.broadcasted_iota(
            jnp.int32, (SUB, SUB), 1
        )
        lags = lags_ref[pl.ds(pl.multiple_of(block * tile, tile), tile)]
        for g in range(tile):
            turned = pltpu.roll(
                jnp.broadcast_to(lags[g : g + 1], (SUB, SUB)), 0, 1, stride=1, stride_axis=0
            )
            toep_ref[g * SUB : (g + 1) * SUB] = jnp.where(below, turned, 0.0).astype(jnp.bfloat16)

    def convolve(block, begin_slot, end_slot):
        span = pl.ds(pl.multiple_of(block * modes, modes), modes)
        leave = split(leave_ref[span])
        reach = split(reach_ref[block, :SUB])
        fade = fade_ref[span]
        skip = skip_ref[:, chan(block)]
        skip = jnp.concatenate([skip, skip], axis=1)
        kernel_taps = [[taps_ref[tap, w : w + 1, chan(block)] for w in range(3)] for tap in range(taps)]

        def segment(slot, carry):
            def filtered(which):
                value = proj_ref[slot, :, which * lanes : (which + 1) * lanes].astype(jnp.float32)
                out = None
                for tap in range(taps):
                    term = kernel_taps[tap][which] * value[HALO - tap : HALO - tap + count]
                    out = term if out is None else out + term
                return out

            query_ref[slot] = filtered(0)
            gated = filtered(1) * filtered(2)
            state = jnp.zeros((modes, lanes), jnp.float32)
            for two in range(count // SUB // 2):
                low, high = 2 * two * SUB, (2 * two + 1) * SUB
                piece = jnp.concatenate([gated[low:high], gated[high : high + SUB]], axis=1)
                spread = jnp.dot(
                    toep_ref[...], piece.astype(jnp.bfloat16), preferred_element_type=jnp.float32
                )
                picked = spread[:SUB]
                for g in range(1, tile):
                    picked = jnp.where(lane == g, spread[g * SUB : (g + 1) * SUB], picked)
                local = skip * piece + picked
                fresh = product_split(leave, split(piece))
                for turn, start in ((0, low), (1, high)):
                    value = local[:, turn * lanes : (turn + 1) * lanes]
                    if start:
                        value = value + product_split(reach, split(state))
                    base_ref[slot, start : start + SUB] = value
                    state = fade * state + jnp.where(
                        diagonal, fresh[:, turn * lanes : (turn + 1) * lanes], 0.0
                    )
            compact = state[:order]
            for g in range(1, tile):
                compact = compact + state[g * order : (g + 1) * order]
            all_ref[block, team, slot] = compact
            return carry

        lax.fori_loop(begin_slot, end_slot, segment, 0)

    def teammate(d):
        there = lax.rem(team + d, depth)
        return there, {
            "seq": index_of(2 * (there // 2) + parity, lax.rem(there, 2), core)
        }

    def shares(block):
        return [
            remote(
                all_ref.at[block, team], all_ref.at[block, team],
                share_send.at[block, d - 1], share_recv.at[block, d - 1], teammate(d)[1],
            )
            for d in range(1, depth)
        ]

    def share_waits(block):
        return [
            remote(
                all_ref.at[block, lax.rem(team - d + depth, depth)],
                all_ref.at[block, lax.rem(team - d + depth, depth)],
                share_send.at[block, d - 1], share_recv.at[block, d - 1], teammate(d)[1],
            )
            for d in range(1, depth)
        ]

    def colleague(d):
        there, which = z ^ (d // 2), (1 - core if d % 2 else core)
        return 2 * lax.rem(there, 2) + which, {"seq": index_of(there, x, which)}

    def combine(block):
        for copy in share_waits(block):
            copy.wait_recv()
        rates = mode_ref[block]
        reach = split(reach_ref[block])

        def segment(slot, carry):
            here = index_of(z - parity + slot // 2, x, lax.rem(slot, 2))

            def member(n, entering):
                for other in range(4):
                    ahead = here - 1 - index_of(
                        2 * (n // 2) + other // 2, lax.rem(n, 2), other % 2
                    )
                    far = (count * jnp.maximum(ahead, 0)).astype(jnp.float32)
                    weight = jnp.where(ahead >= 0, jnp.exp(-rates * far), 0.0)
                    entering = entering + weight * all_ref[block, n, other]
                return entering

            entering = lax.fori_loop(0, depth, member, jnp.zeros((order, lanes), jnp.float32))
            carried = product_split(reach, split(fanned(entering, width, order)))
            mix_ref[block, slot] = (query_ref[slot] * (base_ref[slot] + carried)).astype(mix_ref.dtype)
            return carry

        lax.fori_loop(0, 4, segment, 0)
        full_ref[0, block, own_slot] = mix_ref[block, own_slot]

    def roles(block):
        return [
            remote(
                mix_ref.at[block, colleague(d)[0]], full_ref.at[0, block, own_slot],
                role_send.at[block, d - 1], role_recv.at[block, d - 1], colleague(d)[1],
            )
            for d in (2, 3, 1)
        ]

    def role_waits(block):
        return [
            remote(
                full_ref.at[0, block, colleague(d)[0]], full_ref.at[0, block, colleague(d)[0]],
                role_send.at[block, d - 1], role_recv.at[block, d - 1], colleague(d)[1],
            )
            for d in range(1, 4)
        ]

    def overs(block, n):
        which = colleague(n)[0]
        return [
            remote(
                full_ref.at[0, block, which], full_ref.at[d, block, which],
                over_send.at[block, 4 * (d - 1) + n], over_recv.at[block, 4 * (d - 1) + n], tps[d - 1],
            )
            for d in range(1, n_tp)
        ]

    def over_waits(block):
        return [
            remote(
                full_ref.at[d, block, colleague(n)[0]], full_ref.at[d, block, colleague(n)[0]],
                over_send.at[block, 4 * (d - 1) + n], over_recv.at[block, 4 * (d - 1) + n], tps[d - 1],
            )
            for n in range(4)
            for d in range(1, n_tp)
        ]

    def send_states(block):
        for copy in shares(block):
            copy.start()

    def send_mix(block):
        for copy in roles(block) + overs(block, 0):
            copy.start()

    def send_over(block):
        for n, copy in enumerate(role_waits(block)):
            copy.wait_recv()
            for across_copy in overs(block, n + 1):
                across_copy.start()

    def stage(block, carry):
        @pl.when(block > 0)
        def _():
            forward_slot(block, 0)
            compute(block - 1, depth - 1)
            prepare(block - 1)
            convolve(block - 1, 0, 4)
            send_states(block - 1)

            @pl.when(block + 1 < blocks)
            def _():
                issue(block + 1)

            forward_slot(block, 1)

        compute(block, 0)
        compute(block, 1)
        for turn in range(2, depth - 1):
            forward_slot(block, turn)
            compute(block, turn)

        @pl.when(block > 0)
        def _():
            combine(block - 1)
            send_mix(block - 1)

        @pl.when(block > 1)
        def _():
            send_over(block - 2)

        return carry

    lax.fori_loop(0, blocks, stage, 0)
    swaps = []
    for piece in range(COLUMN_PIECES):
        for d in range(1, n_tp):
            moved[d, piece].wait_recv()
            swaps.append(swap(d, piece))
    compute(blocks - 1, depth - 1)
    if blocks > 1:
        send_over(blocks - 2)
    loads = []

    def load(source, slot, d):
        chans = blocks * lanes
        copy = pltpu.make_async_copy(
            source, tok_ref.at[slot, pl.ds(0, chans), pl.ds(d * out_cols, out_cols)],
            local_sems.at[1 + 4 * d + slot],
        )
        copy.start()
        loads.append(copy)

    def role_rows(slot):
        return pl.ds(slot * blocks * lanes, blocks * lanes)

    inside = twins + list(across.values())
    for copy in inside:
        copy.wait_send()
    for slot in range(4):
        load(out_ref.at[role_rows(slot), out_span(part)], slot, 0)
    prepare(blocks - 1)
    convolve(blocks - 1, 0, 4)
    send_states(blocks - 1)
    for copy in swaps:
        copy.wait_recv()
    for d in range(1, n_tp):
        for slot in range(4):
            load(wo_ref.at[d - 1, role_rows(slot)], slot, d)
    for copy in loads:
        copy.wait()
    strip = min(4 * SUB, out_cols)

    def project(block, carry):
        for copy in over_waits(block):
            copy.wait_recv()
        pairs = [(d, slot) for d in range(n_tp) for slot in range(4)]
        left = jnp.concatenate([full_ref[d, block, slot] for d, slot in pairs], axis=1)
        span = pl.ds(pl.multiple_of(block * lanes, lanes), lanes)

        def one(n, carry):
            right = jnp.concatenate(
                [
                    tok_ref[slot, span, pl.ds(pl.multiple_of(d * out_cols + n * strip, strip), strip)]
                    for d, slot in pairs
                ],
                axis=0,
            )
            value = jnp.dot(left, right, preferred_element_type=jnp.float32)
            where = pl.ds(pl.multiple_of(n * strip, strip), strip)

            @pl.when(block > 0)
            def _():
                total_ref[:, where] = total_ref[:, where] + value

            @pl.when(block == 0)
            def _():
                total_ref[:, where] = value

            return carry

        lax.fori_loop(0, out_cols // strip, one, 0)
        return carry

    lax.fori_loop(0, half, project, 0)
    combine(blocks - 1)
    send_mix(blocks - 1)
    send_over(blocks - 1)
    lax.fori_loop(half, blocks, project, 0)
    mixed_ref[...] = total_ref[...].astype(mixed_ref.dtype)
    for copy in started:
        if all(copy is not other for other in inside):
            copy.wait_send()

    @pl.when(leads)
    def _():
        for copy in edges():
            copy.wait_send()

    def finish(block, carry):
        first(block).wait_send()
        for hop in hops:
            line(block, hop).wait_send()
            passing(block, hop).wait_send()
        for copy in shares(block) + roles(block):
            copy.wait_send()
        for n in range(4):
            for copy in overs(block, n):
                copy.wait_send()
        return carry

    lax.fori_loop(0, blocks, finish, 0)


def hyena(own, w3, w_out, taps, decay, residue, skip, width):
    size, n_tp = lax.axis_size("seq"), lax.axis_size("tp")
    line, depth = size // 2, size // 4
    count = own.shape[0]
    chans = w3.shape[2] // 4
    lanes = min(BLOCK, chans)
    blocks = chans // lanes
    order = decay.shape[0]
    tile = lanes // width
    tall = HALO + count
    out_cols = w_out.shape[1] // n_tp
    anywhere = pl.BlockSpec(memory_space=pl.ANY)
    near = pl.BlockSpec(memory_space=pltpu.VMEM)
    counts = (
        [1 + 4 * n_tp, blocks] + [(blocks, line)] * 4 + [2, 2] + [2 * n_tp] * 4 + [0, 0]
        + [COLUMN_PIECES * n_tp] * 4 + [4, 2]
        + [(blocks, depth - 1)] * 2 + [(blocks, 3)] * 2 + [(blocks, 4 * n_tp)] * 2
    )
    return pl.pallas_call(
        functools.partial(hyena_kernel, width),
        out_shape=[
            jax.ShapeDtypeStruct((count, out_cols), jnp.bfloat16),
            jax.ShapeDtypeStruct((n_tp - 1, w_out.shape[0], out_cols), w_out.dtype),
        ],
        in_specs=[anywhere] * 3 + [near] * 4,
        out_specs=[near, anywhere],
        scratch_shapes=[
            pltpu.VMEM((blocks * tile, SUB), jnp.float32),
            pltpu.VMEM((blocks * tile * order, SUB), jnp.float32),
            pltpu.VMEM((blocks, count, tile * order), jnp.float32),
            pltpu.VMEM((blocks * tile * order, lanes), jnp.float32),
            pltpu.VMEM((blocks, order, lanes), jnp.float32),
            pltpu.VMEM((4, tall, own.shape[1]), own.dtype),
            pltpu.VMEM((blocks, 3, own.shape[1], lanes), w3.dtype),
            pltpu.VMEM((4, tall, 3 * lanes), jnp.float32),
            pltpu.VMEM((4, tall, 3 * lanes), jnp.bfloat16),
            pltpu.VMEM((tile * SUB, SUB), jnp.bfloat16),
            pltpu.VMEM((4, count, lanes), jnp.float32),
            pltpu.VMEM((4, count, lanes), jnp.float32),
            pltpu.VMEM((blocks, depth, 4, order, lanes), jnp.float32),
            pltpu.VMEM((blocks, 4, count, lanes), jnp.bfloat16),
            pltpu.VMEM((n_tp, blocks, 4, count, lanes), jnp.bfloat16),
            pltpu.VMEM((count, out_cols), jnp.float32),
        ]
        + [pltpu.SemaphoreType.DMA(n if isinstance(n, tuple) else (n,) if n else ()) for n in counts],
        compiler_params=pltpu.CompilerParams(
            collective_id=0, has_side_effects=True, vmem_limit_bytes=60 << 20
        ),
        name="hyena",
    )(own, w3, w_out, taps, decay, residue, skip)[0]


def shards(tokens, w_in, short_taps, decay_rate, residue, skip_gain, w_out):
    return hyena(
        tokens, w_in.transpose(1, 0, 2), w_out, short_taps, decay_rate.T, residue.T,
        skip_gain[None], w_in.shape[2] // decay_rate.shape[0],
    )


def solution(mesh):
    in_specs = (
        P("seq", None),
        P("seq", None, "tp"),
        P(None, None, "tp"),
        P("tp", None),
        P("tp", None),
        P("tp"),
        P("tp", None),
    )
    out_specs = P("seq", "tp")
    return jax.shard_map(shards, mesh=mesh, in_specs=in_specs, out_specs=out_specs, check_vma=False)
```

```python
import functools

import jax
import jax.numpy as jnp
from jax import lax
from jax.experimental import pallas as pl
from jax.experimental.pallas import tpu as pltpu
from jax.sharding import PartitionSpec as P

SUB = 128
BLOCK = 128
COLUMN_PIECES = 8
HALO = 16
MESH = pl.DeviceIdType.MESH


def fanned(state, width, order):
    lanes = state.shape[1]
    tile = lanes // width
    full = jnp.concatenate([state] * tile, axis=0)
    row = lax.broadcasted_iota(jnp.int32, full.shape, 0) // order
    lane = lax.broadcasted_iota(jnp.int32, full.shape, 1) // width
    return jnp.where(row == lane, full, 0.0)


def split(value):
    high = value.astype(jnp.bfloat16)
    return high, (value - high.astype(jnp.float32)).astype(jnp.bfloat16)


def product_split(a, b):
    (ah, al), (bh, bl) = a, b
    dot = functools.partial(jnp.dot, preferred_element_type=jnp.float32)
    return dot(ah, bh) + (dot(ah, bl) + dot(al, bh))


def place():
    size, here = lax.axis_size("seq"), lax.axis_index("seq")
    return here // 4, lax.rem(here // 2, 2), lax.rem(here, 2), size // 4


def index_of(z, x, core):
    return z * 4 + x * 2 + core


def greet(peers):
    barrier = pltpu.get_barrier_semaphore()
    for peer in peers:
        pl.semaphore_signal(barrier, inc=1, device_id=peer, device_id_type=MESH)
    pl.semaphore_wait(barrier, len(peers))


def remote(source, target, send_sem, recv_sem, peer):
    return pltpu.make_async_remote_copy(
        src_ref=source,
        dst_ref=target,
        send_sem=send_sem,
        recv_sem=recv_sem,
        device_id=peer,
        device_id_type=MESH,
    )


def coefficients(
    width, role, decay_ref, residue_ref, lags_ref, leave_ref, reach_ref, fade_ref, mode_ref
):
    order = decay_ref.shape[0]
    groups = decay_ref.shape[1] // 4
    blocks, _, lanes = mode_ref.shape
    count, modes = reach_ref.shape[1:]

    def own(ref):
        whole = ref[...]
        part = whole[:, :groups]
        for n in range(1, 4):
            part = jnp.where(role == n, whole[:, n * groups : (n + 1) * groups], part)
        return part

    rate = own(decay_ref)
    gain = own(residue_ref) * jnp.sqrt(2.0 * rate / order)
    place_in = lax.broadcasted_iota(jnp.int32, (order, SUB), 1)
    back = jnp.where(place_in == 0, 0, SUB - place_in).astype(jnp.float32)
    left = (SUB - 1 - place_in).astype(jnp.float32)
    rows = lax.broadcasted_iota(jnp.int32, (order, modes), 0)
    lane = lax.broadcasted_iota(jnp.int32, (order, modes), 1)
    wide = lax.broadcasted_iota(jnp.int32, (order, lanes), 1) // width
    later = lax.broadcasted_iota(jnp.int32, (count, modes), 0).astype(jnp.float32) + 1.0
    per = lanes // width
    for block in range(blocks):
        by_rate = jnp.zeros((order, modes), jnp.float32)
        by_gain = jnp.zeros((order, modes), jnp.float32)
        by_lane = jnp.zeros((order, lanes), jnp.float32)
        for n in range(per):
            g = block * per + n
            column = rate[:, g : g + 1]
            strength = gain[:, g : g + 1]
            span = slice(g * order, (g + 1) * order)
            lags_ref[g : g + 1] = jnp.sum(strength * jnp.exp(-column * back), axis=0, keepdims=True)
            leave_ref[span] = jnp.exp(-column * left)
            fade_ref[span] = jnp.exp(-jnp.broadcast_to(column, (order, lanes)) * SUB)
            by_rate = jnp.where(lane // order == n, column, by_rate)
            by_gain = jnp.where(lane // order == n, strength, by_gain)
            by_lane = jnp.where(wide == n, column, by_lane)
        mode_ref[block] = by_lane
        pick = rows == lax.rem(lane, order)
        flat = jnp.sum(jnp.where(pick, by_rate, 0.0), axis=0, keepdims=True)
        weight = jnp.sum(jnp.where(pick, by_gain, 0.0), axis=0, keepdims=True)
        reach_ref[block] = weight * jnp.exp(-flat * later)


def hyena_kernel(
    width,
    own_ref, w3_ref, out_ref, taps_ref, decay_ref, residue_ref, skip_ref,
    mixed_ref, wo_ref,
    lags_ref, leave_ref, reach_ref, fade_ref, mode_ref, tok_ref, w_ref, acc_ref, proj_ref, toep_ref, query_ref, base_ref, all_ref, mix_ref, full_ref, total_ref, keep_ref,
    local_sems, own_sems,
    line_send, line_recv, pass_send, pass_recv, pair_send, pair_recv,
    tp_send, tp_recv, core_send, core_recv, early_send, early_recv,
    cols_send, cols_recv, swap_send, swap_recv, halo_send, halo_recv,
    share_send, share_recv, role_send, role_recv, over_send, over_recv,
):
    z, x, core, depth = place()
    parity = lax.rem(z, 2)
    n_tp, part = lax.axis_size("tp"), lax.axis_index("tp")
    size = lax.axis_size("seq")
    mine = index_of(z, x, core)
    side = {"seq": index_of(z, 1 - x, core)}
    twin = {"seq": index_of(z, x, 1 - core)}
    blocks, _, _, lanes = w_ref.shape
    rows = w3_ref.shape[1]
    count = own_ref.shape[0]
    taps = taps_ref.shape[0]
    order = all_ref.shape[3]
    tile = lanes // width
    modes = tile * order

    def on_line(hop):
        there = z ^ hop[0]
        return there, (1 - core if hop[1] else core)

    hops = [(step, other) for step in range(depth) for other in range(2)][1:]
    tps = [{"tp": lax.rem(part + d, n_tp)} for d in range(1, n_tp)]
    greet([{"seq": lax.rem(mine + d, size)} for d in range(1, size)] + tps)

    cols = own_ref.shape[1] // (2 * n_tp)

    def band(which, piece):
        return pl.ds(pl.multiple_of((2 * which + piece) * cols, cols), cols)

    own_slot, mate_slot = 2 * parity + core, 2 * (1 - parity) + core
    body = pl.ds(HALO, count)
    edge = pl.ds(HALO // 2, HALO // 2)
    taken = pltpu.make_async_copy(own_ref, tok_ref.at[own_slot, body], local_sems.at[0])
    started = []

    def begin(*what):
        copy = remote(*what)
        copy.start()
        started.append(copy)
        return copy

    def wide(role, block):
        return w3_ref.at[:, :, pl.ds(pl.multiple_of((role * blocks + block) * lanes, lanes), lanes)]

    def landed(block, source):
        return w_ref.at[block, :, pl.ds(pl.multiple_of(source * rows, rows), rows), :]

    def own_piece(block):
        return pltpu.make_async_copy(wide(own_slot, block), landed(block, mine), own_sems.at[block])

    def first(block):
        return remote(
            wide(own_slot, block), landed(block, mine),
            pass_send.at[block, 0], pass_recv.at[block, 0], side,
        )

    def line(block, hop):
        there, which = on_line(hop)
        index = 2 * hop[0] + hop[1]
        return remote(
            wide(2 * lax.rem(there, 2) + which, block), landed(block, mine),
            line_send.at[block, index], line_recv.at[block, index], {"seq": index_of(there, x, which)},
        )

    def arriving(block, hop):
        there, which = on_line(hop)
        index = 2 * hop[0] + hop[1]
        where = landed(block, index_of(there, x, which))
        return remote(
            where, where, line_send.at[block, index], line_recv.at[block, index],
            {"seq": index_of(there, x, which)},
        )

    def passing(block, hop):
        there, which = on_line(hop)
        index = 2 * hop[0] + hop[1]
        where = landed(block, index_of(there, x, which))
        return remote(where, where, pass_send.at[block, index], pass_recv.at[block, index], side)

    def passed(block, hop):
        there, which = on_line(hop)
        index = 2 * hop[0] + hop[1]
        where = landed(block, index_of(there, 1 - x, which))
        return remote(where, where, pass_send.at[block, index], pass_recv.at[block, index], side)

    def to_pair(piece):
        where = tok_ref.at[own_slot, body, band(part, piece)]
        return begin(
            own_ref.at[:, band(part, piece)], where, pair_send.at[piece], pair_recv.at[piece],
            {"seq": index_of(z ^ 1, x, core)},
        )

    portion = wo_ref.shape[1] // (2 * COLUMN_PIECES)
    out_cols = wo_ref.shape[2]

    def portion_rows(piece):
        return pl.ds(pl.multiple_of((COLUMN_PIECES * core + piece) * portion, portion), portion)

    def out_span(which):
        return pl.ds(pl.multiple_of(which * out_cols, out_cols), out_cols)

    moved = {}

    def columns(pieces):
        for piece in pieces:
            for d in range(1, n_tp):
                slot = COLUMN_PIECES * (d - 1) + piece
                moved[d, piece] = begin(
                    out_ref.at[portion_rows(piece), out_span(lax.rem(part + d, n_tp))],
                    wo_ref.at[d - 1, portion_rows(piece)],
                    cols_send.at[slot], cols_recv.at[slot], tps[d - 1],
                )

    def swap(d, piece):
        slot = COLUMN_PIECES * (d - 1) + piece
        where = wo_ref.at[d - 1, portion_rows(piece)]
        return begin(where, where, swap_send.at[slot], swap_recv.at[slot], twin)

    after = jnp.where(x == 0, z, z + 1)
    leads = (core == 1) & ((x == 0) | (z < depth - 1))

    def edges():
        copies = []
        for n in range(4):
            slot = 2 * lax.rem(after, 2)
            copies.append(remote(
                own_ref.at[pl.ds(count - HALO // 2, HALO // 2)], tok_ref.at[slot, edge],
                halo_send.at[n], halo_recv.at[lax.rem(after, 2)],
                {"seq": index_of(after ^ (n // 2), 1 - x, n % 2)},
            ))
        return copies

    inner = (lax.rem(z, 4) == 1) | (lax.rem(z, 4) == 2)

    def step_of(turn):
        if turn == 0:
            return 0
        return jnp.where(
            inner, (turn + depth - 3) % (depth - 1) + 1, 3 - turn if turn < 3 else turn
        )

    def forward(block, step):
        for other in range(2):
            arriving(block, (step, other)).wait_recv()
            passing(block, (step, other)).start()

    def forward_far(block, carry):
        forward(block, depth - 1)
        return carry

    def forward_slot(block, turn):
        outer = 2 - turn if turn < 2 else turn + 1

        @pl.when(jnp.logical_not(inner) | (turn < depth - 2))
        def _():
            forward(block, jnp.where(inner, turn + 1, outer))

    def near(block, carry):
        arriving(block, (0, 1)).wait_recv()
        passing(block, (0, 1)).start()
        return carry

    def begin_own(block, carry):
        own_piece(block).start()
        first(block).start()
        line(block, (0, 1)).start()
        return carry

    def issue_step(block, step):
        for other in range(2):
            line(block, (step, other)).start()

    def issue(block, begin_step=1):
        for step in range(begin_step, depth - 1):
            issue_step(block, step)

        @pl.when(jnp.logical_not(inner))
        def _():
            issue_step(block, depth - 1)

    def issue_far(block, carry):
        issue_step(block, depth - 1)
        return carry

    paired = [to_pair(0), to_pair(1)]
    columns(range(2))
    lax.fori_loop(0, blocks, begin_own, 0)

    @pl.when(leads)
    def _():
        for copy in edges():
            copy.start()

    @pl.when(inner)
    def _():
        lax.fori_loop(0, blocks, issue_far, 0)
        issue_step(0, 1)

    @pl.when(jnp.logical_not(inner))
    def _():
        issue(0)

    early = begin(own_ref, tok_ref.at[own_slot, body], early_send, early_recv, twin)
    taken.start()
    chans = blocks * lanes

    def role_rows(slot):
        return pl.ds(slot * chans, chans)

    kept = [
        pltpu.make_async_copy(
            out_ref.at[role_rows(slot), out_span(part)], keep_ref.at[slot], local_sems.at[1 + slot]
        )
        for slot in range(4)
    ]
    for copy in kept:
        copy.start()
    total_ref[...] = jnp.zeros_like(total_ref)
    twins, across = [], {}

    def to_twin(which, piece, d):
        where = tok_ref.at[mate_slot, body, band(which, piece)]
        slot = 2 * d + piece
        twins.append(begin(where, where, core_send.at[slot], core_recv.at[slot], twin))

    def pair_on(piece):
        paired[piece].wait_recv()
        where = tok_ref.at[mate_slot, body, band(part, piece)]
        for d in range(1, n_tp):
            slot = 2 * (d - 1) + piece
            across[d, piece] = begin(
                where, where, tp_send.at[slot], tp_recv.at[slot], tps[d - 1]
            )
        to_twin(part, piece, 0)

    lax.fori_loop(0, blocks, near, 0)
    coefficients(
        width, own_slot, decay_ref, residue_ref, lags_ref, leave_ref, reach_ref, fade_ref, mode_ref
    )
    half = blocks // 2

    @pl.when(inner)
    def _():
        lax.fori_loop(0, half, forward_far, 0)

    pair_on(0)

    @pl.when(inner)
    def _():
        lax.fori_loop(half, blocks, forward_far, 0)

    pair_on(1)
    columns(range(2, COLUMN_PIECES))

    @pl.when(inner)
    def _():
        for n in range(2, depth - 1):
            issue_step(0, n)

    if blocks > 1:
        issue(1)

    def tokens_on(piece):
        for d in range(1, n_tp):
            across[d, piece].wait_recv()
            to_twin(lax.rem(part - d + n_tp, n_tp), piece, d)

    tokens_on(0)
    forward_slot(0, 0)
    forward_slot(0, 1)
    tokens_on(1)
    taken.wait()
    for copy in kept:
        copy.wait()
    for copy in [early] + twins:
        copy.wait_recv()
    for p in range(2):
        starts = (z - parity + p == 0) & (x == 0)

        @pl.when(starts)
        def _():
            tok_ref[2 * p, HALO // 2 : HALO] = jnp.zeros(
                (HALO // 2, tok_ref.shape[2]), tok_ref.dtype
            )

        @pl.when(jnp.logical_not(starts))
        def _():
            where = tok_ref.at[2 * p, edge]
            remote(where, where, halo_send.at[0], halo_recv.at[p], side).wait_recv()

        tok_ref[2 * p + 1, HALO // 2 : HALO] = tok_ref[2 * p, HALO // 2 + count : HALO + count]

    depth_rows = 4 * rows

    def compute(block, turn):
        step = step_of(turn)

        if turn == 0:
            own_piece(block).wait()

        for other in range(2):
            passed(block, (step, other)).wait_recv()
        span = pl.ds(pl.multiple_of((z ^ step) * depth_rows, depth_rows), depth_rows)

        def one(slot, carry):
            right = jnp.concatenate([w_ref[block, p, span, :] for p in range(3)], axis=1)
            value = jnp.dot(tok_ref[slot, :, span], right, preferred_element_type=jnp.float32)

            acc_ref[slot] = value if turn == 0 else acc_ref[slot] + value
            return carry

        lax.fori_loop(0, 4, one, 0)

        if turn == depth - 1:

            def put(slot, carry):
                proj_ref[slot] = acc_ref[slot].astype(proj_ref.dtype)
                return carry

            lax.fori_loop(0, 4, put, 0)

    team = (z // 2) * 2 + x
    lane = lax.broadcasted_iota(jnp.int32, (SUB, 2 * lanes), 1)
    lane = lax.rem(lane, lanes) // width
    diagonal = (
        lax.broadcasted_iota(jnp.int32, (modes, lanes), 0) // order
        == lax.broadcasted_iota(jnp.int32, (modes, lanes), 1) // width
    )

    def chan(block):
        return pl.ds(pl.multiple_of((own_slot * blocks + block) * lanes, lanes), lanes)

    def prepare(block):
        below = lax.broadcasted_iota(jnp.int32, (SUB, SUB), 0) >= lax.broadcasted_iota(
            jnp.int32, (SUB, SUB), 1
        )
        lags = lags_ref[pl.ds(pl.multiple_of(block * tile, tile), tile)]
        for g in range(tile):
            turned = pltpu.roll(
                jnp.broadcast_to(lags[g : g + 1], (SUB, SUB)), 0, 1, stride=1, stride_axis=0
            )
            toep_ref[g * SUB : (g + 1) * SUB] = jnp.where(below, turned, 0.0).astype(jnp.bfloat16)

    def convolve(block, begin_slot, end_slot):
        span = pl.ds(pl.multiple_of(block * modes, modes), modes)
        leave = split(leave_ref[span])
        reach = split(reach_ref[block, :SUB])
        fade = fade_ref[span]
        skip = skip_ref[:, chan(block)]
        skip = jnp.concatenate([skip, skip], axis=1)
        kernel_taps = [[taps_ref[tap, w : w + 1, chan(block)] for w in range(3)] for tap in range(taps)]

        def segment(slot, carry):
            def filtered(which):
                value = proj_ref[slot, :, which * lanes : (which + 1) * lanes].astype(jnp.float32)
                out = None
                for tap in range(taps):
                    term = kernel_taps[tap][which] * value[HALO - tap : HALO - tap + count]
                    out = term if out is None else out + term
                return out

            query_ref[slot] = filtered(0)
            gated = filtered(1) * filtered(2)
            state = jnp.zeros((modes, lanes), jnp.float32)
            for two in range(count // SUB // 2):
                low, high = 2 * two * SUB, (2 * two + 1) * SUB
                piece = jnp.concatenate([gated[low:high], gated[high : high + SUB]], axis=1)
                spread = jnp.dot(
                    toep_ref[...], piece.astype(jnp.bfloat16), preferred_element_type=jnp.float32
                )
                picked = spread[:SUB]
                for g in range(1, tile):
                    picked = jnp.where(lane == g, spread[g * SUB : (g + 1) * SUB], picked)
                local = skip * piece + picked
                fresh = product_split(leave, split(piece))
                for turn, start in ((0, low), (1, high)):
                    value = local[:, turn * lanes : (turn + 1) * lanes]
                    if start:
                        value = value + product_split(reach, split(state))
                    base_ref[slot, start : start + SUB] = value
                    state = fade * state + jnp.where(
                        diagonal, fresh[:, turn * lanes : (turn + 1) * lanes], 0.0
                    )
            compact = state[:order]
            for g in range(1, tile):
                compact = compact + state[g * order : (g + 1) * order]
            all_ref[block, team, slot] = compact
            return carry

        lax.fori_loop(begin_slot, end_slot, segment, 0)

    def teammate(d):
        there = lax.rem(team + d, depth)
        return there, {
            "seq": index_of(2 * (there // 2) + parity, lax.rem(there, 2), core)
        }

    def shares(block):
        return [
            remote(
                all_ref.at[block, team], all_ref.at[block, team],
                share_send.at[block, d - 1], share_recv.at[block, d - 1], teammate(d)[1],
            )
            for d in range(1, depth)
        ]

    def share_waits(block):
        return [
            remote(
                all_ref.at[block, lax.rem(team - d + depth, depth)],
                all_ref.at[block, lax.rem(team - d + depth, depth)],
                share_send.at[block, d - 1], share_recv.at[block, d - 1], teammate(d)[1],
            )
            for d in range(1, depth)
        ]

    def colleague(d):
        there, which = z ^ (d // 2), (1 - core if d % 2 else core)
        return 2 * lax.rem(there, 2) + which, {"seq": index_of(there, x, which)}

    def combine(block):
        for copy in share_waits(block):
            copy.wait_recv()
        rates = mode_ref[block]
        reach = split(reach_ref[block])

        def segment(slot, carry):
            here = index_of(z - parity + slot // 2, x, lax.rem(slot, 2))

            def member(n, entering):
                for other in range(4):
                    ahead = here - 1 - index_of(
                        2 * (n // 2) + other // 2, lax.rem(n, 2), other % 2
                    )
                    far = (count * jnp.maximum(ahead, 0)).astype(jnp.float32)
                    weight = jnp.where(ahead >= 0, jnp.exp(-rates * far), 0.0)
                    entering = entering + weight * all_ref[block, n, other]
                return entering

            entering = lax.fori_loop(0, depth, member, jnp.zeros((order, lanes), jnp.float32))
            carried = product_split(reach, split(fanned(entering, width, order)))
            mix_ref[block, slot] = (query_ref[slot] * (base_ref[slot] + carried)).astype(mix_ref.dtype)
            return carry

        lax.fori_loop(0, 4, segment, 0)
        full_ref[0, block, own_slot] = mix_ref[block, own_slot]

    def roles(block):
        return [
            remote(
                mix_ref.at[block, colleague(d)[0]], full_ref.at[0, block, own_slot],
                role_send.at[block, d - 1], role_recv.at[block, d - 1], colleague(d)[1],
            )
            for d in (2, 3, 1)
        ]

    def role_waits(block):
        return [
            remote(
                full_ref.at[0, block, colleague(d)[0]], full_ref.at[0, block, colleague(d)[0]],
                role_send.at[block, d - 1], role_recv.at[block, d - 1], colleague(d)[1],
            )
            for d in range(1, 4)
        ]

    def overs(block, n):
        which = colleague(n)[0]
        return [
            remote(
                full_ref.at[0, block, which], full_ref.at[d, block, which],
                over_send.at[block, 4 * (d - 1) + n], over_recv.at[block, 4 * (d - 1) + n], tps[d - 1],
            )
            for d in range(1, n_tp)
        ]

    def over_waits(block):
        return [
            remote(
                full_ref.at[d, block, colleague(n)[0]], full_ref.at[d, block, colleague(n)[0]],
                over_send.at[block, 4 * (d - 1) + n], over_recv.at[block, 4 * (d - 1) + n], tps[d - 1],
            )
            for n in range(4)
            for d in range(1, n_tp)
        ]

    def send_states(block):
        for copy in shares(block):
            copy.start()

    def send_mix(block):
        for copy in roles(block) + overs(block, 0):
            copy.start()

    def send_over(block):
        for n, copy in enumerate(role_waits(block)):
            copy.wait_recv()
            for across_copy in overs(block, n + 1):
                across_copy.start()

    strip = min(4 * SUB, out_cols)

    def project(block, parts, store=None):
        pairs = [(d, slot) for d in parts for slot in range(4)]
        left = jnp.concatenate([full_ref[d, block, slot] for d, slot in pairs], axis=1)
        span = pl.ds(pl.multiple_of(block * lanes, lanes), lanes)

        def one(n, carry):
            where = pl.ds(pl.multiple_of(n * strip, strip), strip)
            right = jnp.concatenate(
                [
                    tok_ref[slot, span, pl.ds(pl.multiple_of(d * out_cols + n * strip, strip), strip)]
                    if d else keep_ref[slot, span, where]
                    for d, slot in pairs
                ],
                axis=0,
            )
            value = total_ref[:, where] + jnp.dot(left, right, preferred_element_type=jnp.float32)
            if store is None:
                total_ref[:, where] = value
            else:
                store[:, where] = value.astype(store.dtype)
            return carry

        lax.fori_loop(0, out_cols // strip, one, 0)

    def project_far(block, store=None):
        for copy in over_waits(block):
            copy.wait_recv()
        project(block, range(1, n_tp), store)

    def stage(block, carry):
        @pl.when(block > 0)
        def _():
            prepare(block - 1)
            forward_slot(block, 0)
            compute(block - 1, depth - 1)
            convolve(block - 1, 0, 4)
            send_states(block - 1)

            @pl.when(block + 1 < blocks)
            def _():
                issue(block + 1)

            forward_slot(block, 1)

        compute(block, 0)
        compute(block, 1)
        for turn in range(2, depth - 1):
            forward_slot(block, turn)
            compute(block, turn)

        @pl.when(block > 0)
        def _():
            combine(block - 1)
            send_mix(block - 1)

        @pl.when(block > 1)
        def _():
            send_over(block - 2)
            project(block - 2, [0])

        return carry

    lax.fori_loop(0, blocks, stage, 0)
    swaps = []
    for piece in range(COLUMN_PIECES):
        for d in range(1, n_tp):
            moved[d, piece].wait_recv()
            swaps.append(swap(d, piece))
    last = blocks - 1
    prepare(last)
    compute(last, depth - 1)
    if last:
        send_over(last - 1)
    inside = twins + list(across.values())
    for copy in inside:
        copy.wait_send()
    for copy in swaps:
        copy.wait_recv()
    loads = [
        pltpu.make_async_copy(
            wo_ref.at[d - 1, role_rows(slot)],
            tok_ref.at[slot, pl.ds(0, chans), pl.ds(d * out_cols, out_cols)],
            local_sems.at[1 + 4 * d + slot],
        )
        for d in range(1, n_tp)
        for slot in range(4)
    ]
    for copy in loads:
        copy.start()
    convolve(last, 0, 4)
    send_states(last)
    if last:
        project(last - 1, [0])
    combine(last)
    send_mix(last)
    for copy in loads:
        copy.wait()
    for block in range(min(last, 2)):
        project_far(block)
    send_over(last)
    project(last, [0])
    for block in range(min(last, 2), last):
        project_far(block)
    project_far(last, mixed_ref)
    for copy in started:
        if all(copy is not other for other in inside):
            copy.wait_send()

    @pl.when(leads)
    def _():
        for copy in edges():
            copy.wait_send()

    def finish(block, carry):
        first(block).wait_send()
        for hop in hops:
            line(block, hop).wait_send()
            passing(block, hop).wait_send()
        for copy in shares(block) + roles(block):
            copy.wait_send()
        for n in range(4):
            for copy in overs(block, n):
                copy.wait_send()
        return carry

    lax.fori_loop(0, blocks, finish, 0)


def hyena(own, w3, w_out, taps, decay, residue, skip, width):
    size, n_tp = lax.axis_size("seq"), lax.axis_size("tp")
    line, depth = size // 2, size // 4
    count = own.shape[0]
    chans = w3.shape[2] // 4
    lanes = min(BLOCK, chans)
    blocks = chans // lanes
    order = decay.shape[0]
    tile = lanes // width
    tall = HALO + count
    out_cols = w_out.shape[1] // n_tp
    anywhere = pl.BlockSpec(memory_space=pl.ANY)
    near = pl.BlockSpec(memory_space=pltpu.VMEM)
    counts = (
        [1 + 4 * n_tp, blocks] + [(blocks, line)] * 4 + [2, 2] + [2 * n_tp] * 4 + [0, 0]
        + [COLUMN_PIECES * n_tp] * 4 + [4, 2]
        + [(blocks, depth - 1)] * 2 + [(blocks, 3)] * 2 + [(blocks, 4 * n_tp)] * 2
    )
    return pl.pallas_call(
        functools.partial(hyena_kernel, width),
        out_shape=[
            jax.ShapeDtypeStruct((count, out_cols), jnp.bfloat16),
            jax.ShapeDtypeStruct((n_tp - 1, w_out.shape[0], out_cols), w_out.dtype),
        ],
        in_specs=[anywhere] * 3 + [near] * 4,
        out_specs=[near, anywhere],
        scratch_shapes=[
            pltpu.VMEM((blocks * tile, SUB), jnp.float32),
            pltpu.VMEM((blocks * tile * order, SUB), jnp.float32),
            pltpu.VMEM((blocks, count, tile * order), jnp.float32),
            pltpu.VMEM((blocks * tile * order, lanes), jnp.float32),
            pltpu.VMEM((blocks, order, lanes), jnp.float32),
            pltpu.VMEM((4, tall, own.shape[1]), own.dtype),
            pltpu.VMEM((blocks, 3, own.shape[1], lanes), w3.dtype),
            pltpu.VMEM((4, tall, 3 * lanes), jnp.float32),
            pltpu.VMEM((4, tall, 3 * lanes), jnp.bfloat16),
            pltpu.VMEM((tile * SUB, SUB), jnp.bfloat16),
            pltpu.VMEM((4, count, lanes), jnp.float32),
            pltpu.VMEM((4, count, lanes), jnp.float32),
            pltpu.VMEM((blocks, depth, 4, order, lanes), jnp.float32),
            pltpu.VMEM((blocks, 4, count, lanes), jnp.bfloat16),
            pltpu.VMEM((n_tp, blocks, 4, count, lanes), jnp.bfloat16),
            pltpu.VMEM((count, out_cols), jnp.float32),
            pltpu.VMEM((4, blocks * lanes, out_cols), w_out.dtype),
        ]
        + [pltpu.SemaphoreType.DMA(n if isinstance(n, tuple) else (n,) if n else ()) for n in counts],
        compiler_params=pltpu.CompilerParams(
            collective_id=0, has_side_effects=True, vmem_limit_bytes=61 << 20
        ),
        name="hyena",
    )(own, w3, w_out, taps, decay, residue, skip)[0]


def shards(tokens, w_in, short_taps, decay_rate, residue, skip_gain, w_out):
    return hyena(
        tokens, w_in.transpose(1, 0, 2), w_out, short_taps, decay_rate.T, residue.T,
        skip_gain[None], w_in.shape[2] // decay_rate.shape[0],
    )


def solution(mesh):
    in_specs = (
        P("seq", None),
        P("seq", None, "tp"),
        P(None, None, "tp"),
        P("tp", None),
        P("tp", None),
        P("tp"),
        P("tp", None),
    )
    out_specs = P("seq", "tp")
    return jax.shard_map(shards, mesh=mesh, in_specs=in_specs, out_specs=out_specs, check_vma=False)
```

```python
import functools

import jax
import jax.numpy as jnp
from jax import lax
from jax.experimental import pallas as pl
from jax.experimental.pallas import tpu as pltpu
from jax.sharding import PartitionSpec as P

SUB = 128
BLOCK = 128
COLUMN_PIECES = 8
PIECES = 4
HALO = 16
MESH = pl.DeviceIdType.MESH


def fanned(state, width, order):
    lanes = state.shape[1]
    tile = lanes // width
    full = jnp.concatenate([state] * tile, axis=0)
    row = lax.broadcasted_iota(jnp.int32, full.shape, 0) // order
    lane = lax.broadcasted_iota(jnp.int32, full.shape, 1) // width
    return jnp.where(row == lane, full, 0.0)


def split(value):
    high = value.astype(jnp.bfloat16)
    return high, (value - high.astype(jnp.float32)).astype(jnp.bfloat16)


def product_split(a, b):
    (ah, al), (bh, bl) = a, b
    dot = functools.partial(jnp.dot, preferred_element_type=jnp.float32)
    return dot(ah, bh) + (dot(ah, bl) + dot(al, bh))


def place():
    size, here = lax.axis_size("seq"), lax.axis_index("seq")
    return here // 4, lax.rem(here // 2, 2), lax.rem(here, 2), size // 4


def index_of(z, x, core):
    return z * 4 + x * 2 + core


def greet(peers):
    barrier = pltpu.get_barrier_semaphore()
    for peer in peers:
        pl.semaphore_signal(barrier, inc=1, device_id=peer, device_id_type=MESH)
    pl.semaphore_wait(barrier, len(peers))


def remote(source, target, send_sem, recv_sem, peer):
    return pltpu.make_async_remote_copy(
        src_ref=source,
        dst_ref=target,
        send_sem=send_sem,
        recv_sem=recv_sem,
        device_id=peer,
        device_id_type=MESH,
    )


def coefficients(
    width, role, decay_ref, residue_ref, lags_ref, leave_ref, reach_ref, fade_ref, mode_ref
):
    order = decay_ref.shape[0]
    groups = decay_ref.shape[1] // 4
    blocks, _, lanes = mode_ref.shape
    count, modes = reach_ref.shape[1:]

    def own(ref):
        whole = ref[...]
        part = whole[:, :groups]
        for n in range(1, 4):
            part = jnp.where(role == n, whole[:, n * groups : (n + 1) * groups], part)
        return part

    rate = own(decay_ref)
    gain = own(residue_ref) * jnp.sqrt(2.0 * rate / order)
    place_in = lax.broadcasted_iota(jnp.int32, (order, SUB), 1)
    back = jnp.where(place_in == 0, 0, SUB - place_in).astype(jnp.float32)
    left = (SUB - 1 - place_in).astype(jnp.float32)
    rows = lax.broadcasted_iota(jnp.int32, (order, modes), 0)
    lane = lax.broadcasted_iota(jnp.int32, (order, modes), 1)
    wide = lax.broadcasted_iota(jnp.int32, (order, lanes), 1) // width
    later = lax.broadcasted_iota(jnp.int32, (count, modes), 0).astype(jnp.float32) + 1.0
    per = lanes // width
    for block in range(blocks):
        by_rate = jnp.zeros((order, modes), jnp.float32)
        by_gain = jnp.zeros((order, modes), jnp.float32)
        by_lane = jnp.zeros((order, lanes), jnp.float32)
        for n in range(per):
            g = block * per + n
            column = rate[:, g : g + 1]
            strength = gain[:, g : g + 1]
            span = slice(g * order, (g + 1) * order)
            lags_ref[g : g + 1] = jnp.sum(strength * jnp.exp(-column * back), axis=0, keepdims=True)
            leave_ref[span] = jnp.exp(-column * left)
            fade_ref[span] = jnp.exp(-jnp.broadcast_to(column, (order, lanes)) * SUB)
            by_rate = jnp.where(lane // order == n, column, by_rate)
            by_gain = jnp.where(lane // order == n, strength, by_gain)
            by_lane = jnp.where(wide == n, column, by_lane)
        mode_ref[block] = by_lane
        pick = rows == lax.rem(lane, order)
        flat = jnp.sum(jnp.where(pick, by_rate, 0.0), axis=0, keepdims=True)
        weight = jnp.sum(jnp.where(pick, by_gain, 0.0), axis=0, keepdims=True)
        reach_ref[block] = weight * jnp.exp(-flat * later)


def hyena_kernel(
    width,
    own_ref, w3_ref, out_ref, taps_ref, decay_ref, residue_ref, skip_ref,
    mixed_ref, wo_ref,
    lags_ref, leave_ref, reach_ref, fade_ref, mode_ref, tok_ref, w_ref, acc_ref, proj_ref, toep_ref, query_ref, base_ref, all_ref, mix_ref, full_ref, total_ref, keep_ref,
    local_sems, own_sems,
    line_send, line_recv, pass_send, pass_recv, pair_send, pair_recv,
    tp_send, tp_recv, core_send, core_recv, early_send, early_recv,
    cols_send, cols_recv, swap_send, swap_recv, halo_send, halo_recv,
    share_send, share_recv, role_send, role_recv, over_send, over_recv,
):
    z, x, core, depth = place()
    parity = lax.rem(z, 2)
    n_tp, part = lax.axis_size("tp"), lax.axis_index("tp")
    size = lax.axis_size("seq")
    mine = index_of(z, x, core)
    side = {"seq": index_of(z, 1 - x, core)}
    twin = {"seq": index_of(z, x, 1 - core)}
    blocks, _, _, lanes = w_ref.shape
    rows = w3_ref.shape[1]
    count = own_ref.shape[0]
    taps = taps_ref.shape[0]
    order = all_ref.shape[3]
    tile = lanes // width
    modes = tile * order

    def on_line(hop):
        there = z ^ hop[0]
        return there, (1 - core if hop[1] else core)

    hops = [(step, other) for step in range(depth) for other in range(2)][1:]
    tps = [{"tp": lax.rem(part + d, n_tp)} for d in range(1, n_tp)]
    greet([{"seq": lax.rem(mine + d, size)} for d in range(1, size)] + tps)

    cols = own_ref.shape[1] // (PIECES * n_tp)

    def band(which, piece):
        return pl.ds(pl.multiple_of((PIECES * which + piece) * cols, cols), cols)

    own_slot, mate_slot = 2 * parity + core, 2 * (1 - parity) + core
    body = pl.ds(HALO, count)
    edge = pl.ds(HALO // 2, HALO // 2)
    taken = pltpu.make_async_copy(own_ref, tok_ref.at[own_slot, body], local_sems.at[0])
    started = []

    def begin(*what):
        copy = remote(*what)
        copy.start()
        started.append(copy)
        return copy

    def wide(role, block):
        return w3_ref.at[:, :, pl.ds(pl.multiple_of((role * blocks + block) * lanes, lanes), lanes)]

    def landed(block, source):
        return w_ref.at[block, :, pl.ds(pl.multiple_of(source * rows, rows), rows), :]

    def own_piece(block):
        return pltpu.make_async_copy(wide(own_slot, block), landed(block, mine), own_sems.at[block])

    def first(block):
        return remote(
            wide(own_slot, block), landed(block, mine),
            pass_send.at[block, 0], pass_recv.at[block, 0], side,
        )

    def line(block, hop):
        there, which = on_line(hop)
        index = 2 * hop[0] + hop[1]
        return remote(
            wide(2 * lax.rem(there, 2) + which, block), landed(block, mine),
            line_send.at[block, index], line_recv.at[block, index], {"seq": index_of(there, x, which)},
        )

    def arriving(block, hop):
        there, which = on_line(hop)
        index = 2 * hop[0] + hop[1]
        where = landed(block, index_of(there, x, which))
        return remote(
            where, where, line_send.at[block, index], line_recv.at[block, index],
            {"seq": index_of(there, x, which)},
        )

    def passing(block, hop):
        there, which = on_line(hop)
        index = 2 * hop[0] + hop[1]
        where = landed(block, index_of(there, x, which))
        return remote(where, where, pass_send.at[block, index], pass_recv.at[block, index], side)

    def passed(block, hop):
        there, which = on_line(hop)
        index = 2 * hop[0] + hop[1]
        where = landed(block, index_of(there, 1 - x, which))
        return remote(where, where, pass_send.at[block, index], pass_recv.at[block, index], side)

    def to_pair(piece):
        where = tok_ref.at[own_slot, body, band(part, piece)]
        return begin(
            own_ref.at[:, band(part, piece)], where, pair_send.at[piece], pair_recv.at[piece],
            {"seq": index_of(z ^ 1, x, core)},
        )

    portion = wo_ref.shape[1] // (2 * COLUMN_PIECES)
    out_cols = wo_ref.shape[2]

    def portion_rows(piece):
        return pl.ds(pl.multiple_of((COLUMN_PIECES * core + piece) * portion, portion), portion)

    def out_span(which):
        return pl.ds(pl.multiple_of(which * out_cols, out_cols), out_cols)

    moved = {}

    def columns(pieces):
        for piece in pieces:
            for d in range(1, n_tp):
                slot = COLUMN_PIECES * (d - 1) + piece
                moved[d, piece] = begin(
                    out_ref.at[portion_rows(piece), out_span(lax.rem(part + d, n_tp))],
                    wo_ref.at[d - 1, portion_rows(piece)],
                    cols_send.at[slot], cols_recv.at[slot], tps[d - 1],
                )

    def swap(d, piece):
        slot = COLUMN_PIECES * (d - 1) + piece
        where = wo_ref.at[d - 1, portion_rows(piece)]
        return begin(where, where, swap_send.at[slot], swap_recv.at[slot], twin)

    after = jnp.where(x == 0, z, z + 1)
    leads = (core == 1) & ((x == 0) | (z < depth - 1))

    def edges():
        copies = []
        for n in range(4):
            slot = 2 * lax.rem(after, 2)
            copies.append(remote(
                own_ref.at[pl.ds(count - HALO // 2, HALO // 2)], tok_ref.at[slot, edge],
                halo_send.at[n], halo_recv.at[lax.rem(after, 2)],
                {"seq": index_of(after ^ (n // 2), 1 - x, n % 2)},
            ))
        return copies

    inner = (lax.rem(z, 4) == 1) | (lax.rem(z, 4) == 2)

    def step_of(turn):
        if turn == 0:
            return 0
        return jnp.where(
            inner, (turn + depth - 3) % (depth - 1) + 1, 3 - turn if turn < 3 else turn
        )

    def forward(block, step):
        for other in range(2):
            arriving(block, (step, other)).wait_recv()
            passing(block, (step, other)).start()

    def forward_far(block, carry):
        forward(block, depth - 1)
        return carry

    def forward_slot(block, turn):
        outer = 2 - turn if turn < 2 else turn + 1

        @pl.when(jnp.logical_not(inner) | (turn < depth - 2))
        def _():
            forward(block, jnp.where(inner, turn + 1, outer))

    def near(block, carry):
        arriving(block, (0, 1)).wait_recv()
        passing(block, (0, 1)).start()
        return carry

    def begin_own(block, carry):
        own_piece(block).start()
        first(block).start()
        line(block, (0, 1)).start()
        return carry

    def issue_step(block, step):
        for other in range(2):
            line(block, (step, other)).start()

    def issue(block, begin_step=1):
        for step in range(begin_step, depth - 1):
            issue_step(block, step)

        @pl.when(jnp.logical_not(inner))
        def _():
            issue_step(block, depth - 1)

    def issue_far(block, carry):
        issue_step(block, depth - 1)
        return carry

    paired = [to_pair(piece) for piece in range(PIECES)]
    columns(range(1))
    lax.fori_loop(0, blocks, begin_own, 0)

    @pl.when(leads)
    def _():
        for copy in edges():
            copy.start()

    @pl.when(inner)
    def _():
        lax.fori_loop(0, blocks, issue_far, 0)
        issue_step(0, 1)

    @pl.when(jnp.logical_not(inner))
    def _():
        issue(0)

    early = begin(own_ref, tok_ref.at[own_slot, body], early_send, early_recv, twin)
    taken.start()
    chans = blocks * lanes

    def role_rows(slot):
        return pl.ds(slot * chans, chans)

    kept = [
        pltpu.make_async_copy(
            out_ref.at[role_rows(slot), out_span(part)], keep_ref.at[slot], local_sems.at[1 + slot]
        )
        for slot in range(4)
    ]
    for copy in kept:
        copy.start()
    total_ref[...] = jnp.zeros_like(total_ref)
    twins, across = [], {}

    def to_twin(which, piece, d):
        where = tok_ref.at[mate_slot, body, band(which, piece)]
        slot = PIECES * d + piece
        twins.append(begin(where, where, core_send.at[slot], core_recv.at[slot], twin))

    def pair_on(piece):
        paired[piece].wait_recv()
        where = tok_ref.at[mate_slot, body, band(part, piece)]
        for d in range(1, n_tp):
            slot = PIECES * (d - 1) + piece
            across[d, piece] = begin(
                where, where, tp_send.at[slot], tp_recv.at[slot], tps[d - 1]
            )
        to_twin(part, piece, 0)

    lax.fori_loop(0, blocks, near, 0)
    coefficients(
        width, own_slot, decay_ref, residue_ref, lags_ref, leave_ref, reach_ref, fade_ref, mode_ref
    )
    half = blocks // 2

    @pl.when(inner)
    def _():
        lax.fori_loop(0, half, forward_far, 0)

    for piece in range(PIECES // 2):
        pair_on(piece)

    @pl.when(inner)
    def _():
        lax.fori_loop(half, blocks, forward_far, 0)

    for piece in range(PIECES // 2, PIECES):
        pair_on(piece)
    columns(range(1, COLUMN_PIECES))

    @pl.when(inner)
    def _():
        for n in range(2, depth - 1):
            issue_step(0, n)

    if blocks > 1:
        issue(1)

    def tokens_on(piece):
        for d in range(1, n_tp):
            across[d, piece].wait_recv()
            to_twin(lax.rem(part - d + n_tp, n_tp), piece, d)

    for piece in range(PIECES // 2):
        tokens_on(piece)
    forward_slot(0, 0)
    forward_slot(0, 1)
    for piece in range(PIECES // 2, PIECES):
        tokens_on(piece)
    taken.wait()
    for copy in kept:
        copy.wait()
    for copy in [early] + twins:
        copy.wait_recv()
    for p in range(2):
        starts = (z - parity + p == 0) & (x == 0)

        @pl.when(starts)
        def _():
            tok_ref[2 * p, HALO // 2 : HALO] = jnp.zeros(
                (HALO // 2, tok_ref.shape[2]), tok_ref.dtype
            )

        @pl.when(jnp.logical_not(starts))
        def _():
            where = tok_ref.at[2 * p, edge]
            remote(where, where, halo_send.at[0], halo_recv.at[p], side).wait_recv()

        tok_ref[2 * p + 1, HALO // 2 : HALO] = tok_ref[2 * p, HALO // 2 + count : HALO + count]

    depth_rows = 4 * rows

    def compute(block, turn):
        step = step_of(turn)

        if turn == 0:
            own_piece(block).wait()

        for other in range(2):
            passed(block, (step, other)).wait_recv()
        span = pl.ds(pl.multiple_of((z ^ step) * depth_rows, depth_rows), depth_rows)

        def one(slot, carry):
            right = jnp.concatenate([w_ref[block, p, span, :] for p in range(3)], axis=1)
            value = jnp.dot(tok_ref[slot, :, span], right, preferred_element_type=jnp.float32)

            acc_ref[slot] = value if turn == 0 else acc_ref[slot] + value
            return carry

        lax.fori_loop(0, 4, one, 0)

        if turn == depth - 1:

            def put(slot, carry):
                proj_ref[slot] = acc_ref[slot].astype(proj_ref.dtype)
                return carry

            lax.fori_loop(0, 4, put, 0)

    team = (z // 2) * 2 + x
    lane = lax.broadcasted_iota(jnp.int32, (SUB, 2 * lanes), 1)
    lane = lax.rem(lane, lanes) // width
    diagonal = (
        lax.broadcasted_iota(jnp.int32, (modes, lanes), 0) // order
        == lax.broadcasted_iota(jnp.int32, (modes, lanes), 1) // width
    )

    def chan(block):
        return pl.ds(pl.multiple_of((own_slot * blocks + block) * lanes, lanes), lanes)

    def prepare(block):
        below = lax.broadcasted_iota(jnp.int32, (SUB, SUB), 0) >= lax.broadcasted_iota(
            jnp.int32, (SUB, SUB), 1
        )
        lags = lags_ref[pl.ds(pl.multiple_of(block * tile, tile), tile)]
        for g in range(tile):
            turned = pltpu.roll(
                jnp.broadcast_to(lags[g : g + 1], (SUB, SUB)), 0, 1, stride=1, stride_axis=0
            )
            toep_ref[g * SUB : (g + 1) * SUB] = jnp.where(below, turned, 0.0).astype(jnp.bfloat16)

    def convolve(block, begin_slot, end_slot):
        span = pl.ds(pl.multiple_of(block * modes, modes), modes)
        leave = split(leave_ref[span])
        reach = split(reach_ref[block, :SUB])
        fade = fade_ref[span]
        skip = skip_ref[:, chan(block)]
        skip = jnp.concatenate([skip, skip], axis=1)
        kernel_taps = [[taps_ref[tap, w : w + 1, chan(block)] for w in range(3)] for tap in range(taps)]

        def segment(slot, carry):
            def filtered(which):
                value = proj_ref[slot, :, which * lanes : (which + 1) * lanes].astype(jnp.float32)
                out = None
                for tap in range(taps):
                    term = kernel_taps[tap][which] * value[HALO - tap : HALO - tap + count]
                    out = term if out is None else out + term
                return out

            query_ref[slot] = filtered(0)
            gated = filtered(1) * filtered(2)
            state = jnp.zeros((modes, lanes), jnp.float32)
            for two in range(count // SUB // 2):
                low, high = 2 * two * SUB, (2 * two + 1) * SUB
                piece = jnp.concatenate([gated[low:high], gated[high : high + SUB]], axis=1)
                spread = jnp.dot(
                    toep_ref[...], piece.astype(jnp.bfloat16), preferred_element_type=jnp.float32
                )
                picked = spread[:SUB]
                for g in range(1, tile):
                    picked = jnp.where(lane == g, spread[g * SUB : (g + 1) * SUB], picked)
                local = skip * piece + picked
                fresh = product_split(leave, split(piece))
                for turn, start in ((0, low), (1, high)):
                    value = local[:, turn * lanes : (turn + 1) * lanes]
                    if start:
                        value = value + product_split(reach, split(state))
                    base_ref[slot, start : start + SUB] = value
                    state = fade * state + jnp.where(
                        diagonal, fresh[:, turn * lanes : (turn + 1) * lanes], 0.0
                    )
            compact = state[:order]
            for g in range(1, tile):
                compact = compact + state[g * order : (g + 1) * order]
            all_ref[block, team, slot] = compact
            return carry

        lax.fori_loop(begin_slot, end_slot, segment, 0)

    def teammate(d):
        there = lax.rem(team + d, depth)
        return there, {
            "seq": index_of(2 * (there // 2) + parity, lax.rem(there, 2), core)
        }

    def shares(block):
        return [
            remote(
                all_ref.at[block, team], all_ref.at[block, team],
                share_send.at[block, d - 1], share_recv.at[block, d - 1], teammate(d)[1],
            )
            for d in range(1, depth)
        ]

    def share_waits(block):
        return [
            remote(
                all_ref.at[block, lax.rem(team - d + depth, depth)],
                all_ref.at[block, lax.rem(team - d + depth, depth)],
                share_send.at[block, d - 1], share_recv.at[block, d - 1], teammate(d)[1],
            )
            for d in range(1, depth)
        ]

    def colleague(d):
        there, which = z ^ (d // 2), (1 - core if d % 2 else core)
        return 2 * lax.rem(there, 2) + which, {"seq": index_of(there, x, which)}

    def combine(block):
        for copy in share_waits(block):
            copy.wait_recv()
        rates = mode_ref[block]
        reach = split(reach_ref[block])

        def segment(slot, carry):
            here = index_of(z - parity + slot // 2, x, lax.rem(slot, 2))

            def member(n, entering):
                for other in range(4):
                    ahead = here - 1 - index_of(
                        2 * (n // 2) + other // 2, lax.rem(n, 2), other % 2
                    )
                    far = (count * jnp.maximum(ahead, 0)).astype(jnp.float32)
                    weight = jnp.where(ahead >= 0, jnp.exp(-rates * far), 0.0)
                    entering = entering + weight * all_ref[block, n, other]
                return entering

            entering = lax.fori_loop(0, depth, member, jnp.zeros((order, lanes), jnp.float32))
            carried = product_split(reach, split(fanned(entering, width, order)))
            mix_ref[block, slot] = (query_ref[slot] * (base_ref[slot] + carried)).astype(mix_ref.dtype)
            return carry

        lax.fori_loop(0, 4, segment, 0)
        full_ref[0, block, own_slot] = mix_ref[block, own_slot]

    def roles(block):
        return [
            remote(
                mix_ref.at[block, colleague(d)[0]], full_ref.at[0, block, own_slot],
                role_send.at[block, d - 1], role_recv.at[block, d - 1], colleague(d)[1],
            )
            for d in (2, 3, 1)
        ]

    def role_waits(block):
        return [
            remote(
                full_ref.at[0, block, colleague(d)[0]], full_ref.at[0, block, colleague(d)[0]],
                role_send.at[block, d - 1], role_recv.at[block, d - 1], colleague(d)[1],
            )
            for d in range(1, 4)
        ]

    def overs(block, n):
        which = colleague(n)[0]
        return [
            remote(
                full_ref.at[0, block, which], full_ref.at[d, block, which],
                over_send.at[block, 4 * (d - 1) + n], over_recv.at[block, 4 * (d - 1) + n], tps[d - 1],
            )
            for d in range(1, n_tp)
        ]

    def over_waits(block):
        return [
            remote(
                full_ref.at[d, block, colleague(n)[0]], full_ref.at[d, block, colleague(n)[0]],
                over_send.at[block, 4 * (d - 1) + n], over_recv.at[block, 4 * (d - 1) + n], tps[d - 1],
            )
            for n in range(4)
            for d in range(1, n_tp)
        ]

    def send_states(block):
        for copy in shares(block):
            copy.start()

    def send_mix(block):
        for copy in roles(block) + overs(block, 0):
            copy.start()

    def send_over(block):
        for n, copy in enumerate(role_waits(block)):
            copy.wait_recv()
            for across_copy in overs(block, n + 1):
                across_copy.start()

    strip = min(4 * SUB, out_cols)

    def project(block, parts, store=None):
        pairs = [(d, slot) for d in parts for slot in range(4)]
        left = jnp.concatenate([full_ref[d, block, slot] for d, slot in pairs], axis=1)
        span = pl.ds(pl.multiple_of(block * lanes, lanes), lanes)

        def one(n, carry):
            where = pl.ds(pl.multiple_of(n * strip, strip), strip)
            right = jnp.concatenate(
                [
                    tok_ref[slot, span, pl.ds(pl.multiple_of(d * out_cols + n * strip, strip), strip)]
                    if d else keep_ref[slot, span, where]
                    for d, slot in pairs
                ],
                axis=0,
            )
            value = total_ref[:, where] + jnp.dot(left, right, preferred_element_type=jnp.float32)
            if store is None:
                total_ref[:, where] = value
            else:
                store[:, where] = value.astype(store.dtype)
            return carry

        lax.fori_loop(0, out_cols // strip, one, 0)

    def project_far(block, store=None):
        for copy in over_waits(block):
            copy.wait_recv()
        project(block, range(1, n_tp), store)

    def stage(block, carry):
        @pl.when(block > 0)
        def _():
            prepare(block - 1)
            forward_slot(block, 0)
            compute(block - 1, depth - 1)
            convolve(block - 1, 0, 4)
            send_states(block - 1)

            @pl.when(block + 1 < blocks)
            def _():
                issue(block + 1)

            forward_slot(block, 1)

        compute(block, 0)
        compute(block, 1)
        for turn in range(2, depth - 1):
            forward_slot(block, turn)
            compute(block, turn)

        @pl.when(block > 0)
        def _():
            combine(block - 1)
            send_mix(block - 1)

        @pl.when(block > 1)
        def _():
            send_over(block - 2)
            project(block - 2, [0])

        return carry

    lax.fori_loop(0, blocks, stage, 0)
    swaps = []
    for piece in range(COLUMN_PIECES):
        for d in range(1, n_tp):
            moved[d, piece].wait_recv()
            swaps.append(swap(d, piece))
    last = blocks - 1
    prepare(last)
    compute(last, depth - 1)
    if last:
        send_over(last - 1)
    inside = twins + list(across.values())
    for copy in inside:
        copy.wait_send()
    for copy in swaps:
        copy.wait_recv()
    loads = [
        pltpu.make_async_copy(
            wo_ref.at[d - 1, role_rows(slot)],
            tok_ref.at[slot, pl.ds(0, chans), pl.ds(d * out_cols, out_cols)],
            local_sems.at[1 + 4 * d + slot],
        )
        for d in range(1, n_tp)
        for slot in range(4)
    ]
    for copy in loads:
        copy.start()
    convolve(last, 0, 4)
    send_states(last)
    if last:
        project(last - 1, [0])
    combine(last)
    send_mix(last)
    for copy in loads:
        copy.wait()
    for block in range(min(last, 2)):
        project_far(block)
    send_over(last)
    project(last, [0])
    for block in range(min(last, 2), last):
        project_far(block)
    project_far(last, mixed_ref)
    for copy in started:
        if all(copy is not other for other in inside):
            copy.wait_send()

    @pl.when(leads)
    def _():
        for copy in edges():
            copy.wait_send()

    def finish(block, carry):
        first(block).wait_send()
        for hop in hops:
            line(block, hop).wait_send()
            passing(block, hop).wait_send()
        for copy in shares(block) + roles(block):
            copy.wait_send()
        for n in range(4):
            for copy in overs(block, n):
                copy.wait_send()
        return carry

    lax.fori_loop(0, blocks, finish, 0)


def hyena(own, w3, w_out, taps, decay, residue, skip, width):
    size, n_tp = lax.axis_size("seq"), lax.axis_size("tp")
    line, depth = size // 2, size // 4
    count = own.shape[0]
    chans = w3.shape[2] // 4
    lanes = min(BLOCK, chans)
    blocks = chans // lanes
    order = decay.shape[0]
    tile = lanes // width
    tall = HALO + count
    out_cols = w_out.shape[1] // n_tp
    anywhere = pl.BlockSpec(memory_space=pl.ANY)
    near = pl.BlockSpec(memory_space=pltpu.VMEM)
    counts = (
        [1 + 4 * n_tp, blocks] + [(blocks, line)] * 4 + [PIECES, PIECES] + [PIECES * n_tp] * 4 + [0, 0]
        + [COLUMN_PIECES * n_tp] * 4 + [4, 2]
        + [(blocks, depth - 1)] * 2 + [(blocks, 3)] * 2 + [(blocks, 4 * n_tp)] * 2
    )
    return pl.pallas_call(
        functools.partial(hyena_kernel, width),
        out_shape=[
            jax.ShapeDtypeStruct((count, out_cols), jnp.bfloat16),
            jax.ShapeDtypeStruct((n_tp - 1, w_out.shape[0], out_cols), w_out.dtype),
        ],
        in_specs=[anywhere] * 3 + [near] * 4,
        out_specs=[near, anywhere],
        scratch_shapes=[
            pltpu.VMEM((blocks * tile, SUB), jnp.float32),
            pltpu.VMEM((blocks * tile * order, SUB), jnp.float32),
            pltpu.VMEM((blocks, count, tile * order), jnp.float32),
            pltpu.VMEM((blocks * tile * order, lanes), jnp.float32),
            pltpu.VMEM((blocks, order, lanes), jnp.float32),
            pltpu.VMEM((4, tall, own.shape[1]), own.dtype),
            pltpu.VMEM((blocks, 3, own.shape[1], lanes), w3.dtype),
            pltpu.VMEM((4, tall, 3 * lanes), jnp.float32),
            pltpu.VMEM((4, tall, 3 * lanes), jnp.bfloat16),
            pltpu.VMEM((tile * SUB, SUB), jnp.bfloat16),
            pltpu.VMEM((4, count, lanes), jnp.float32),
            pltpu.VMEM((4, count, lanes), jnp.float32),
            pltpu.VMEM((blocks, depth, 4, order, lanes), jnp.float32),
            pltpu.VMEM((blocks, 4, count, lanes), jnp.bfloat16),
            pltpu.VMEM((n_tp, blocks, 4, count, lanes), jnp.bfloat16),
            pltpu.VMEM((count, out_cols), jnp.float32),
            pltpu.VMEM((4, blocks * lanes, out_cols), w_out.dtype),
        ]
        + [pltpu.SemaphoreType.DMA(n if isinstance(n, tuple) else (n,) if n else ()) for n in counts],
        compiler_params=pltpu.CompilerParams(
            collective_id=0, has_side_effects=True, vmem_limit_bytes=61 << 20
        ),
        name="hyena",
    )(own, w3, w_out, taps, decay, residue, skip)[0]


def shards(tokens, w_in, short_taps, decay_rate, residue, skip_gain, w_out):
    return hyena(
        tokens, w_in.transpose(1, 0, 2), w_out, short_taps, decay_rate.T, residue.T,
        skip_gain[None], w_in.shape[2] // decay_rate.shape[0],
    )


def solution(mesh):
    in_specs = (
        P("seq", None),
        P("seq", None, "tp"),
        P(None, None, "tp"),
        P("tp", None),
        P("tp", None),
        P("tp"),
        P("tp", None),
    )
    out_specs = P("seq", "tp")
    return jax.shard_map(shards, mesh=mesh, in_specs=in_specs, out_specs=out_specs, check_vma=False)
```
